32 devices in a mesh: tm: 16 (over z, y, core), rows: 2 (over x).
Axes of the slice: x: 2, y: 2, z: 4, core: 2. Of those that a mesh axis runs over, the one named last changes fastest.
Arguments:
- latents: bfloat16 [128, 4, 32, 512], P('tm', 'rows'), may hold values from -6 to 6
- clip_ids: int32 [128], replicated, may hold values from 0 to 24, never falling along the last dimension, each value on 1 to 9 neighbouring positions
- gain_in: float32 [512], replicated, may hold values from 0.25 to 1.75
- w_space: bfloat16 [3, 3, 512, 512], P(None, None, None, 'tm'), may hold values from -0.09375 to 0.09375
- w_time: bfloat16 [3, 512, 512], replicated, may hold values from -0.15625 to 0.15625
- gain_attn: float32 [512], replicated, may hold values from 0.25 to 1.75
- w_qkv: bfloat16 [512, 1536], replicated, may hold values from -0.25 to 0.25
- w_out: bfloat16 [512, 512], replicated, may hold values from -0.25 to 0.25
Outputs:
- block_out: bfloat16 [128, 4, 32, 512], P('tm', 'rows')
The draws below stay inside these ranges and needn't reach their ends.
Inputs may be any that keep to these rules, and one draw needn't show every extreme that they name: `clip_ids`: clip numbers never fall along time; each clip has 1 to 9 frames and some clip has exactly 9.
All inputs are finite; a program needn't handle non-finite values.
Results may differ from the reference program's by a relative error of at most 0.0085.
Values may be sent and summed in bfloat16 or wider, within the bound.
No kernel may reach another device: no remote copies, remote signals or barrier semaphores. Data moves between devices by JAX's collectives and lax.ppermute only.
A program may use at most 64 MiB of HBM per device.

```python
import math
import jax
import jax.numpy as jnp
import numpy as np
from jax import lax

C = 512
TD = 8
LW = 32
MOST = 9
LT = 128
HT = 4
N_TM = 16


def block_levels(key, extent, shards, least, high):
    def one(axis_at, blocks):
        draws = jax.random.uniform(jax.random.fold_in(jax.random.fold_in(key, 6), axis_at), (blocks,), jnp.float32, least / len(shards), high / len(shards))
        return jnp.repeat(jnp.exp(draws), extent[axis_at] // blocks).reshape((-1,) + (1,) * (len(extent) - axis_at - 1))

    loudness = one(*shards[0])
    for cut in shards[1:]:
        loudness = loudness * one(*cut)
    return loudness


def split_up(count, total, reach, lean):
    portions = [(1 << 20) // math.isqrt(grade ** lean) + 1 for grade in range(2, count + 1)]
    spare, given = total - reach - (count - 1), [1] * (count - 1)
    while spare > 0:
        candidates = [i for i in range(count - 1) if given[i] < reach]
        mass, budget = sum([portions[i] for i in candidates]), spare
        for i in candidates:
            extra = min(reach - given[i], max(1, budget * portions[i] // mass), spare)
            given[i] = given[i] + extra
            spare = spare - extra
    return np.array([reach] + given)


def ragged(rng, number_of, total, reach, slope):
    if number_of == 2:
        one = jax.random.randint(rng, (), max(1, total - reach), min(reach, total - 1) + 1)
        return jnp.stack([one, total - one])
    tallies = jnp.asarray(split_up(number_of, total, reach, slope), jnp.int32)
    pairs = (number_of - 1) // 2
    source_of, sink = tallies[1:1 + 2 * pairs:2], tallies[2:2 + 2 * pairs:2]
    room = jnp.minimum(source_of - 1, reach - sink)
    passed = jax.random.randint(jax.random.fold_in(rng, 1), (pairs,), 0, 1 << 20) % (room + 1)
    tallies = tallies.at[1:1 + 2 * pairs:2].set(source_of - passed).at[2:2 + 2 * pairs:2].set(sink + passed)
    return tallies[jax.random.permutation(jax.random.fold_in(rng, 2), number_of)]


def bell_draw(rng, dims, scale, bound, shards=(), kind=jnp.bfloat16):
    drawn = scale * jax.random.normal(rng, dims, jnp.float32)
    if shards:
        drawn = drawn * block_levels(rng, dims, shards, -0.22, 0.18)
    return jnp.clip(drawn, -bound, bound).astype(kind)


def setup_inputs(seed: int = 0) -> dict:
    key_of = jax.random.split(jax.random.key(seed), 9)
    latents = bell_draw(key_of[0], (LT, HT, LW, C), 1.0, 6.0, ((0, 16), (1, 2)))
    clip_ids = jnp.searchsorted(jnp.cumsum(ragged(key_of[1], TD * N_TM // 5, LT, MOST, 0)), jnp.arange(LT), side="right").astype(jnp.int32)
    gain_in = jnp.clip(1.0 + 0.15 * jax.random.normal(key_of[2], (C,), jnp.float32), 0.25, 1.75)
    w_space = bell_draw(key_of[3], (3, 3, C, C), (9 * C) ** -0.5, 0.09375, ((3, 16),))
    w_time = bell_draw(key_of[4], (3, C, C), (3 * C) ** -0.5, 0.15625)
    gain_attn = jnp.clip(1.0 + 0.15 * jax.random.normal(key_of[5], (C,), jnp.float32), 0.25, 1.75)
    w_qkv = bell_draw(key_of[6], (C, 3 * C), C ** -0.5, 0.25)
    w_out = bell_draw(key_of[7], (C, C), C ** -0.5, 0.25)
    return {"latents": latents, "clip_ids": clip_ids, "gain_in": gain_in, "w_space": w_space, "w_time": w_time, "gain_attn": gain_attn, "w_qkv": w_qkv, "w_out": w_out}


def rms_scale(values, gain):
    floats = values.astype(jnp.float32)
    scale = lax.rsqrt(lax.optimization_barrier(jnp.mean(floats * floats, axis=-1, keepdims=True)) + 1e-06)
    return (floats * scale * gain).astype(jnp.bfloat16)

def reference(latents, clip_ids, gain_in, w_space, w_time, gain_attn, w_qkv, w_out):
    frames, height, width, chans = latents.shape
    normed = rms_scale(latents, gain_in)

    def spatial(frame):
        padded = jnp.pad(frame, ((1, 1), (1, 1), (0, 0)))
        total = jnp.zeros((height * width, chans), jnp.float32)
        for dy in range(3):
            for dx in range(3):
                window = padded[dy:dy + height, dx:dx + width].reshape(-1, chans)
                total = total + jnp.dot(window, w_space[dy, dx], preferred_element_type=jnp.float32)
        return jax.nn.silu(total).astype(jnp.bfloat16).reshape(height, width, chans)
    acts = lax.map(spatial, normed)
    act_pad = jnp.concatenate([jnp.zeros((2, height, width, chans), jnp.bfloat16), acts], 0)
    seg_pad = jnp.concatenate([jnp.full((2,), -1, jnp.int32), clip_ids.astype(jnp.int32)])

    def temporal(index):
        own = lax.dynamic_index_in_dim(seg_pad, index + 2, 0, keepdims=False)
        total = lax.dynamic_index_in_dim(latents, index, 0, keepdims=False).astype(jnp.float32).reshape(-1, chans)
        for back in range(3):
            source = lax.dynamic_index_in_dim(act_pad, index + 2 - back, 0, keepdims=False)
            other = lax.dynamic_index_in_dim(seg_pad, index + 2 - back, 0, keepdims=False)
            keep = (other == own).astype(jnp.bfloat16)
            total = total + jnp.dot((source * keep).reshape(-1, chans), w_time[back], preferred_element_type=jnp.float32)
        return total.astype(jnp.bfloat16).reshape(height, width, chans)
    resid = lax.map(temporal, jnp.arange(frames, dtype=jnp.int32))

    def context(carry, item):
        running, number, previous = carry
        frame, segment = item
        same = segment == previous
        running = jnp.where(same, running, jnp.float32(0.0)) + frame.astype(jnp.float32)
        number = jnp.where(same, number, jnp.float32(0.0)) + jnp.float32(1.0)
        mixed_frame = (frame.astype(jnp.float32) + running / number).astype(jnp.bfloat16)
        return ((running, number, segment), mixed_frame)
    start = (jnp.zeros((height, width, chans), jnp.float32), jnp.float32(0.0), jnp.int32(-1))
    _, mixed = lax.scan(context, start, (resid, clip_ids.astype(jnp.int32)))

    def attend(frame):
        tokens = rms_scale(frame, gain_attn).reshape(-1, chans)
        qkv = jnp.dot(tokens, w_qkv, preferred_element_type=jnp.float32).astype(jnp.bfloat16)
        query = qkv[:, :chans]
        key = qkv[:, chans:2 * chans]
        value = qkv[:, 2 * chans:]
        scores = jnp.dot(query, key.T, preferred_element_type=jnp.float32) * chans ** (-0.5)
        probs = jax.nn.softmax(scores, axis=-1).astype(jnp.bfloat16)
        attended = jnp.dot(probs, value, preferred_element_type=jnp.float32).astype(jnp.bfloat16)
        result = frame.astype(jnp.float32).reshape(-1, chans) + jnp.dot(attended, w_out, preferred_element_type=jnp.float32)
        return result.astype(jnp.bfloat16).reshape(height, width, chans)
    return lax.map(attend, mixed)
```

```python
import functools

import jax
import jax.numpy as jnp
from jax import lax
from jax.experimental import pallas as pl
from jax.experimental.pallas import tpu as pltpu
from jax.sharding import PartitionSpec as P

LONGEST = 9
VMEM = pl.BlockSpec(memory_space=pltpu.VMEM)
SMEM = pl.BlockSpec(memory_space=pltpu.SMEM)
PARAMS = pltpu.CompilerParams(vmem_limit_bytes=60 << 20)
F32 = jnp.float32
BF16 = jnp.bfloat16


def dot(a, b):
    return jnp.dot(a, b, preferred_element_type=F32)


def dot_t(a, b):
    return lax.dot_general(a, b, (((1,), (1,)), ((), ())), preferred_element_type=F32)


def spot_of(device, count):
    z, y = device // 4, (device // 2) % 2
    return z + y * (count // 2 - 1 - 2 * z)


def device_at(spot, core, count):
    y = spot // (count // 4)
    return (spot + y * (count // 2 - 1 - 2 * spot)) * 4 + y * 2 + core


def ring_pairs(count):
    ring = count // 2
    pairs = []
    for spot in range(ring):
        pairs.append((device_at(spot, 0, count), device_at((spot + 1) % ring, 0, count)))
        pairs.append((device_at(spot, 1, count), device_at((spot - 1) % ring, 1, count)))
    return pairs


def gather_ring(own, count):
    ring = ring_pairs(count)
    cores = [(i, i ^ 1) for i in range(count)]
    last = count // 4
    twin = lax.ppermute(own, "tm", cores)
    found = [(own, (0, 0, 0)), (twin, (0, 0, 1))]
    straight, crossed = own, twin
    for step in range(1, last + 1):
        straight = lax.ppermute(straight, "tm", ring)
        found.append((straight, (step, 0, 0)))
        found.append((lax.ppermute(straight, "tm", cores), (step, 1, 1)))
        if step < last:
            crossed = lax.ppermute(crossed, "tm", ring)
            found.append((crossed, (step, 0, 1)))
            found.append((lax.ppermute(crossed, "tm", cores), (step, 1, 0)))
    return found


def shard_owner(tag, device, count):
    step, swapped, flip = tag
    core = device % 2
    ring = count // 2
    away = (1 - 2 * core) * ((1 - 2 * swapped) * step)
    spot = (spot_of(device, count) - away + ring) % ring
    return device_at(spot, (core + flip) % 2, count)


def prepare_kernel(tags, *refs):
    *parts, gain_ref, time_ref, wide_ref, lat_ref, head_ref, tail_ref = refs
    frames, rows, width, chans = parts[0].shape
    groups = len(parts)
    mine = lax.axis_index("rows")
    gain = gain_ref[...]
    column = lax.broadcasted_iota(jnp.int32, (rows * width, 1), 0) % width
    edge = jnp.zeros((width, 3 * chans), BF16)
    for frame in range(frames):
        wide_ref[frame, 0] = edge
        wide_ref[frame, groups * rows + 1] = edge
    for at, part in enumerate(parts):
        first = at * rows
        if groups == 2:
            first = (mine if at == 0 else 1 - mine) * rows
        for frame in range(frames):
            raw = part[frame]
            lat_ref[frame, pl.ds(first, rows)] = raw
            x = raw.reshape(rows * width, chans).astype(F32)
            y = x * lax.rsqrt(jnp.mean(x * x, axis=-1, keepdims=True) + 1e-06) * gain
            before = jnp.where(column == 0, 0.0, pltpu.roll(y, 1, 0))
            after = jnp.where(column == width - 1, 0.0, pltpu.roll(y, rows * width - 1, 0))
            for dx, v in enumerate((before, y, after)):
                wide_ref[frame, pl.ds(first + 1, rows), :, dx * chans : (dx + 1) * chans] = v.astype(
                    BF16
                ).reshape(rows, width, chans)
    block = chans // len(tags)
    device = lax.axis_index("tm")
    for slot, tag in enumerate(tags):
        owner = tag
        if isinstance(tag, tuple):
            owner = shard_owner(tag, device, len(tags))
        source = pl.ds(pl.multiple_of(owner * block, block), block)
        to_ref, at = head_ref, slot * block
        if at >= head_ref.shape[1]:
            to_ref, at = tail_ref, at - head_ref.shape[1]
        for back in range(3):
            to_ref[back, at : at + block] = time_ref[back, source]


def convolve(wide_ref, shards):
    frames, height, width, wide = wide_ref.shape
    height -= 2
    total = None
    for dy in range(3):
        weights = jnp.concatenate(
            [jnp.concatenate([shard[dy, dx] for dx in range(3)], axis=-1) for shard in shards], axis=0
        )
        lhs = wide_ref[:, dy : dy + height].reshape(frames * height * width, wide)
        part = dot_t(lhs, weights)
        total = part if total is None else total + part
    acts = (total * jax.nn.sigmoid(total)).astype(BF16)
    return acts.reshape(frames, height * width, -1)


def keep(flag, values):
    return jnp.where(flag, values, jnp.zeros_like(values))


def temporal(acts, clips, weights, frames):
    first = lax.axis_index("tm") * frames
    spots, width = acts[0].shape
    lines = []
    for t in range(frames):
        line = [acts[t]]
        for back in (1, 2):
            if t < back:
                line.append(jnp.zeros((spots, width), BF16))
            else:
                line.append(keep(clips[first + t - back] == clips[first + t], acts[t - back]))
        lines.append(jnp.concatenate(line, axis=-1))
    lhs = jnp.concatenate(lines, axis=0)
    rhs = jnp.concatenate([weights[k] for k in range(3)], axis=0)
    return dot(lhs, rhs)


def packet_sums(acts, clips, weights, frames, lat=None):
    first = lax.axis_index("tm") * frames
    end = clips.shape[0] - 1
    next0 = clips[jnp.minimum(first + frames, end)]
    next1 = clips[jnp.minimum(first + frames + 1, end)]
    spots, width = acts[0].shape
    sums = [jnp.zeros((spots, width), F32) for _ in range(3)]
    base = None if lat is None else jnp.zeros(lat[0].shape, F32)
    for t in range(frames):
        inside = clips[first + t] == next0
        if lat is not None:
            base = base + keep(inside, lat[t].astype(F32))
        for back in range(min(3, t + 1)):
            both = jnp.logical_and(inside, clips[first + t - back] == next0)
            sums[back] = sums[back] + keep(both, acts[t - back].astype(F32))
    sums = [s.astype(BF16) for s in sums]
    last0 = keep(clips[first + frames - 1] == next0, acts[frames - 1])
    prev0 = keep(clips[first + frames - 2] == next0, acts[frames - 2])
    last1 = keep(clips[first + frames - 1] == next1, acts[frames - 1])
    by0 = dot(sums[0], weights[0])
    by1 = dot(jnp.concatenate([last0, sums[1]], axis=0), weights[1])
    by2 = dot(jnp.concatenate([prev0, last1, sums[2]], axis=0), weights[2])
    total = by0 + by1[spots:] + by2[2 * spots :]
    if base is not None:
        total = total + base
    return by1[:spots] + by2[:spots], by2[spots : 2 * spots], total


def early_kernel(wide_ref, lat_ref, clips, weights, *refs):
    *shards, rest_ref, packet_ref = refs
    frames = wide_ref.shape[0]
    acts = convolve(wide_ref, shards)
    acts = [acts[t] for t in range(frames)]
    lat = [lat_ref[t].reshape(acts[0].shape[0], -1) for t in range(frames)]
    for i, part in enumerate(packet_sums(acts, clips, weights, frames, lat)):
        packet_ref[i] = part
    rest = temporal(acts, clips, weights, frames).reshape(rest_ref.shape)
    for t in range(frames):
        rest_ref[t] = rest[t] + lat[t].astype(F32)


def late_kernel(wide_ref, clips, weights, early_ref, *refs):
    *shards, acts_ref, packet_ref = refs
    frames = wide_ref.shape[0]
    acts = convolve(wide_ref, shards)
    acts_ref[...] = acts
    acts = [acts[t] for t in range(frames)]
    for i, part in enumerate(packet_sums(acts, clips, weights, frames)):
        packet_ref[i] = (early_ref[i] + part).astype(BF16)


def rest_kernel(acts_ref, clips, weights, early_ref, rest_ref):
    frames = acts_ref.shape[0]
    part = temporal([acts_ref[t] for t in range(frames)], clips, weights, frames)
    rest_ref[...] = early_ref[...] + part.reshape(rest_ref.shape)


def attend_kernel(rest_ref, packet_ref, clips, gain_ref, qkv_ref, proj_ref, out_ref, mixed_ref, normed_ref):
    frames, rows, width, chans = out_ref.shape
    height = mixed_ref.shape[1]
    spots = height * width
    own = rows * width
    first = lax.axis_index("tm") * frames
    mine = pl.ds(lax.axis_index("rows") * rows, rows)
    gain = gain_ref[...]

    number = jnp.int32(1)
    for back in range(1, LONGEST):
        at = first - back
        hit = jnp.logical_and(at >= 0, clips[jnp.maximum(at, 0)] == clips[first])
        number = number + hit.astype(jnp.int32)
    running = packet_ref[2].astype(F32)
    for t in range(frames):
        resid = rest_ref[t]
        if t < 2:
            resid = resid + packet_ref[t].astype(F32)
        if t > 0:
            same = clips[first + t] == clips[first + t - 1]
            running = keep(same, running)
            number = jnp.where(same, number + 1, 1)
        running = running + resid
        mixed = (resid + running / jnp.full((1, chans), number.astype(F32))).astype(BF16)
        mixed_ref[t] = mixed.reshape(height, width, chans)
        x = mixed.astype(F32)
        y = x * lax.rsqrt(jnp.mean(x * x, axis=-1, keepdims=True) + 1e-06) * gain
        normed_ref[t] = y.astype(BF16).reshape(height, width, chans)

    query = dot(normed_ref[:, mine].reshape(frames * own, chans), qkv_ref[:, :chans]).astype(BF16)
    both = dot(normed_ref[...].reshape(frames * spots, chans), qkv_ref[:, chans:]).astype(BF16)
    attended = []
    for t in range(frames):
        key = both[t * spots : (t + 1) * spots, :chans]
        value = both[t * spots : (t + 1) * spots, chans:]
        scores = dot_t(query[t * own : (t + 1) * own], key) * chans ** (-0.5)
        weights = jnp.exp(scores - jnp.max(scores, axis=-1, keepdims=True))
        probs = (weights / jnp.sum(weights, axis=-1, keepdims=True)).astype(BF16)
        attended.append(dot(probs, value).astype(BF16))
    result = dot(jnp.concatenate(attended, axis=0), proj_ref[...])
    result = result + mixed_ref[:, mine].reshape(frames * own, chans).astype(F32)
    out_ref[...] = result.astype(BF16).reshape(frames, rows, width, chans)


def local(latents, clip_ids, gain_in, w_space, w_time, gain_attn, w_qkv, w_out):
    frames, rows, width, chans = latents.shape
    groups, count = lax.axis_size("rows"), lax.axis_size("tm")
    height = groups * rows
    spots = height * width
    shape = jax.ShapeDtypeStruct
    assert frames + 1 >= LONGEST

    if groups == 2:
        parts = [latents, lax.ppermute(latents, "rows", [(0, 1), (1, 0)])]
    else:
        everything = lax.all_gather(latents, "rows")
        parts = [everything[i] for i in range(groups)]

    shard = jnp.transpose(w_space, (0, 1, 3, 2))
    if shard.shape[2] % 16 == 0 and count % 8 == 0:
        found = gather_ring(shard, count)
        cut = len(found) // 2
    else:
        whole = lax.all_gather(shard, "tm", axis=2, tiled=True)
        half = chans // 2
        found = [(whole[:, :, :half], 0), (whole[:, :, half:], 1)]
        cut = 1
    shards = [pair[0] for pair in found]
    tags = [pair[1] for pair in found]
    split = cut * (chans // len(tags))

    wide, lat, head, tail = pl.pallas_call(
        functools.partial(prepare_kernel, tags),
        out_shape=(
            shape((frames, height + 2, width, 3 * chans), BF16),
            shape((frames, height, width, chans), BF16),
            shape((3, split, chans), BF16),
            shape((3, chans - split, chans), BF16),
        ),
        in_specs=[VMEM] * (len(parts) + 2),
        out_specs=(VMEM, VMEM, VMEM, VMEM),
        compiler_params=PARAMS,
        name="prepare",
    )(*parts, gain_in.reshape(1, chans), w_time)

    rest, packet = pl.pallas_call(
        early_kernel,
        out_shape=(shape((frames, spots, chans), F32), shape((3, spots, chans), F32)),
        in_specs=[VMEM, VMEM, SMEM, VMEM] + [VMEM] * cut,
        out_specs=(VMEM, VMEM),
        compiler_params=PARAMS,
        name="early",
    )(wide, lat, clip_ids, head, *shards[:cut])
    acts, packet = pl.pallas_call(
        late_kernel,
        out_shape=(shape((frames, spots, chans - split), BF16), shape((3, spots, chans), BF16)),
        in_specs=[VMEM, SMEM, VMEM, VMEM] + [VMEM] * (len(tags) - cut),
        out_specs=(VMEM, VMEM),
        compiler_params=PARAMS,
        name="late",
    )(wide, clip_ids, tail, packet, *shards[cut:])
    packet = lax.ppermute(packet, "tm", [(i, i + 1) for i in range(count - 1)])
    rest = pl.pallas_call(
        rest_kernel,
        out_shape=shape((frames, spots, chans), F32),
        in_specs=[VMEM, SMEM, VMEM, VMEM],
        out_specs=VMEM,
        compiler_params=PARAMS,
        name="rest",
    )(acts, clip_ids, tail, rest)
    return pl.pallas_call(
        attend_kernel,
        out_shape=shape((frames, rows, width, chans), BF16),
        in_specs=[VMEM, VMEM, SMEM, VMEM, VMEM, VMEM],
        out_specs=VMEM,
        scratch_shapes=[
            pltpu.VMEM((frames, height, width, chans), BF16),
            pltpu.VMEM((frames, height, width, chans), BF16),
        ],
        compiler_params=PARAMS,
        name="attend",
    )(rest, packet, clip_ids, gain_attn.reshape(1, chans), w_qkv, w_out)


def solution(mesh):
    placed = (P("tm", "rows", None, None), P(), P(), P(None, None, None, "tm"), P(), P(), P(), P())
    return jax.shard_map(
        local, mesh=mesh, in_specs=placed, out_specs=P("tm", "rows", None, None), check_vma=False
    )
```

```python
import functools

import jax
import jax.numpy as jnp
from jax import lax
from jax.experimental import pallas as pl
from jax.experimental.pallas import tpu as pltpu
from jax.sharding import PartitionSpec as P

LONGEST = 9
VMEM = pl.BlockSpec(memory_space=pltpu.VMEM)
SMEM = pl.BlockSpec(memory_space=pltpu.SMEM)
F32 = jnp.float32
BF16 = jnp.bfloat16


def dot(a, b):
    return jnp.dot(a, b, preferred_element_type=F32)


def dot_t(a, b):
    return lax.dot_general(a, b, (((1,), (1,)), ((), ())), preferred_element_type=F32)


def spot_of(device, count):
    z, y = device // 4, (device // 2) % 2
    return z + y * (count // 2 - 1 - 2 * z)


def device_at(spot, core, count):
    y = spot // (count // 4)
    return (spot + y * (count // 2 - 1 - 2 * spot)) * 4 + y * 2 + core


def ring_pairs(count):
    ring = count // 2
    pairs = []
    for spot in range(ring):
        pairs.append((device_at(spot, 0, count), device_at((spot + 1) % ring, 0, count)))
        pairs.append((device_at(spot, 1, count), device_at((spot - 1) % ring, 1, count)))
    return pairs


def gather_ring(own, count):
    ring = ring_pairs(count)
    cores = [(i, i ^ 1) for i in range(count)]
    last = count // 4
    twin = lax.ppermute(own, "tm", cores)
    found = [(own, (0, 0, 0)), (twin, (0, 0, 1))]
    straight, crossed = own, twin
    for step in range(1, last + 1):
        straight = lax.ppermute(straight, "tm", ring)
        found.append((straight, (step, 0, 0)))
        found.append((lax.ppermute(straight, "tm", cores), (step, 1, 1)))
        if step < last:
            crossed = lax.ppermute(crossed, "tm", ring)
            found.append((crossed, (step, 0, 1)))
            found.append((lax.ppermute(crossed, "tm", cores), (step, 1, 0)))
    return found


def shard_owner(tag, device, count):
    step, swapped, flip = tag
    core = device % 2
    ring = count // 2
    away = (1 - 2 * core) * ((1 - 2 * swapped) * step)
    spot = (spot_of(device, count) - away + ring) % ring
    return device_at(spot, (core + flip) % 2, count)


def prepare_kernel(tags, *refs):
    *parts, gain_ref, time_ref, wide_ref, lat_ref, head_ref, tail_ref = refs
    frames, rows, width, chans = parts[0].shape
    groups = len(parts)
    mine = lax.axis_index("rows")
    gain = gain_ref[...]
    column = lax.broadcasted_iota(jnp.int32, (rows * width, 1), 0) % width
    edge = jnp.zeros((width, 3 * chans), BF16)
    for frame in range(frames):
        wide_ref[frame, 0] = edge
        wide_ref[frame, groups * rows + 1] = edge
    for at, part in enumerate(parts):
        first = at * rows
        if groups == 2:
            first = (mine if at == 0 else 1 - mine) * rows
        for frame in range(frames):
            raw = part[frame]
            lat_ref[frame, pl.ds(first, rows)] = raw
            x = raw.reshape(rows * width, chans).astype(F32)
            y = x * lax.rsqrt(jnp.mean(x * x, axis=-1, keepdims=True) + 1e-06) * gain
            before = jnp.where(column == 0, 0.0, pltpu.roll(y, 1, 0))
            after = jnp.where(column == width - 1, 0.0, pltpu.roll(y, rows * width - 1, 0))
            for dx, v in enumerate((before, y, after)):
                wide_ref[frame, pl.ds(first + 1, rows), :, dx * chans : (dx + 1) * chans] = v.astype(
                    BF16
                ).reshape(rows, width, chans)
    block = chans // len(tags)
    device = lax.axis_index("tm")
    for slot, tag in enumerate(tags):
        owner = tag
        if isinstance(tag, tuple):
            owner = shard_owner(tag, device, len(tags))
        source = pl.ds(pl.multiple_of(owner * block, block), block)
        to_ref, at = head_ref, slot * block
        if at >= head_ref.shape[1]:
            to_ref, at = tail_ref, at - head_ref.shape[1]
        for back in range(3):
            to_ref[back, at : at + block] = time_ref[back, source]


def convolve(wide_ref, shards):
    frames, height, width, wide = wide_ref.shape
    height -= 2
    total = None
    for dy in range(3):
        weights = jnp.concatenate(
            [jnp.concatenate([shard[dy, dx] for dx in range(3)], axis=-1) for shard in shards], axis=0
        )
        lhs = wide_ref[:, dy : dy + height].reshape(frames * height * width, wide)
        part = dot_t(lhs, weights)
        total = part if total is None else total + part
    acts = (total * jax.nn.sigmoid(total)).astype(BF16)
    return acts.reshape(frames, height * width, -1)


def keep(flag, values):
    return jnp.where(flag, values, jnp.zeros_like(values))


def temporal(acts, clips, weights, frames):
    first = lax.axis_index("tm") * frames
    spots, width = acts[0].shape
    lines = []
    for t in range(frames):
        line = [acts[t]]
        for back in (1, 2):
            if t < back:
                line.append(jnp.zeros((spots, width), BF16))
            else:
                line.append(keep(clips[first + t - back] == clips[first + t], acts[t - back]))
        lines.append(jnp.concatenate(line, axis=-1))
    lhs = jnp.concatenate(lines, axis=0)
    rhs = jnp.concatenate([weights[k] for k in range(3)], axis=0)
    return dot(lhs, rhs)


def packet_sums(acts, clips, weights, frames, lat=None):
    first = lax.axis_index("tm") * frames
    end = clips.shape[0] - 1
    next0 = clips[jnp.minimum(first + frames, end)]
    next1 = clips[jnp.minimum(first + frames + 1, end)]
    spots, width = acts[0].shape
    sums = [jnp.zeros((spots, width), F32) for _ in range(3)]
    base = None if lat is None else jnp.zeros(lat[0].shape, F32)
    for t in range(frames):
        inside = clips[first + t] == next0
        if lat is not None:
            base = base + keep(inside, lat[t].astype(F32))
        for back in range(min(3, t + 1)):
            both = jnp.logical_and(inside, clips[first + t - back] == next0)
            sums[back] = sums[back] + keep(both, acts[t - back].astype(F32))
    sums = [s.astype(BF16) for s in sums]
    last0 = keep(clips[first + frames - 1] == next0, acts[frames - 1])
    prev0 = keep(clips[first + frames - 2] == next0, acts[frames - 2])
    last1 = keep(clips[first + frames - 1] == next1, acts[frames - 1])
    by0 = dot(sums[0], weights[0])
    by1 = dot(jnp.concatenate([last0, sums[1]], axis=0), weights[1])
    by2 = dot(jnp.concatenate([prev0, last1, sums[2]], axis=0), weights[2])
    total = by0 + by1[spots:] + by2[2 * spots :]
    if base is not None:
        total = total + base
    return by1[:spots] + by2[:spots], by2[spots : 2 * spots], total


def early_kernel(wide_ref, lat_ref, clips, weights, *refs):
    *shards, rest_ref, packet_ref = refs
    frames = wide_ref.shape[0]
    acts = convolve(wide_ref, shards)
    acts = [acts[t] for t in range(frames)]
    lat = [lat_ref[t].reshape(acts[0].shape[0], -1) for t in range(frames)]
    for i, part in enumerate(packet_sums(acts, clips, weights, frames, lat)):
        packet_ref[i] = part
    rest = temporal(acts, clips, weights, frames).reshape(rest_ref.shape)
    for t in range(frames):
        rest_ref[t] = rest[t] + lat[t].astype(F32)


def late_kernel(wide_ref, clips, weights, early_ref, *refs):
    *shards, acts_ref, packet_ref = refs
    frames = wide_ref.shape[0]
    acts = convolve(wide_ref, shards)
    acts_ref[...] = acts
    acts = [acts[t] for t in range(frames)]
    for i, part in enumerate(packet_sums(acts, clips, weights, frames)):
        packet_ref[i] = (early_ref[i] + part).astype(BF16)


def rest_kernel(acts_ref, clips, weights, early_ref, rest_ref):
    frames = acts_ref.shape[0]
    part = temporal([acts_ref[t] for t in range(frames)], clips, weights, frames)
    rest_ref[...] = early_ref[...] + part.reshape(rest_ref.shape)


def attend_kernel(rest_ref, packet_ref, clips, gain_ref, qkv_ref, proj_ref, out_ref, mixed_ref, normed_ref):
    frames, rows, width, chans = out_ref.shape
    height = mixed_ref.shape[1]
    spots = height * width
    own = rows * width
    first = lax.axis_index("tm") * frames
    mine = pl.ds(lax.axis_index("rows") * rows, rows)
    gain = gain_ref[...]

    number = jnp.int32(1)
    for back in range(1, LONGEST):
        at = first - back
        hit = jnp.logical_and(at >= 0, clips[jnp.maximum(at, 0)] == clips[first])
        number = number + hit.astype(jnp.int32)
    running = packet_ref[2].astype(F32)
    for t in range(frames):
        resid = rest_ref[t]
        if t < 2:
            resid = resid + packet_ref[t].astype(F32)
        if t > 0:
            same = clips[first + t] == clips[first + t - 1]
            running = keep(same, running)
            number = jnp.where(same, number + 1, 1)
        running = running + resid
        mixed = (resid + running / jnp.full((1, chans), number.astype(F32))).astype(BF16)
        mixed_ref[t] = mixed.reshape(height, width, chans)
        x = mixed.astype(F32)
        y = x * lax.rsqrt(jnp.mean(x * x, axis=-1, keepdims=True) + 1e-06) * gain
        normed_ref[t] = y.astype(BF16).reshape(height, width, chans)

    query = dot(normed_ref[:, mine].reshape(frames * own, chans), qkv_ref[:, :chans]).astype(BF16)
    both = dot(normed_ref[...].reshape(frames * spots, chans), qkv_ref[:, chans:]).astype(BF16)
    attended = []
    for t in range(frames):
        key = both[t * spots : (t + 1) * spots, :chans]
        value = both[t * spots : (t + 1) * spots, chans:]
        scores = dot_t(query[t * own : (t + 1) * own], key) * chans ** (-0.5)
        weights = jnp.exp(scores - jnp.max(scores, axis=-1, keepdims=True))
        probs = (weights / jnp.sum(weights, axis=-1, keepdims=True)).astype(BF16)
        attended.append(dot(probs, value).astype(BF16))
    result = dot(jnp.concatenate(attended, axis=0), proj_ref[...])
    result = result + mixed_ref[:, mine].reshape(frames * own, chans).astype(F32)
    out_ref[...] = result.astype(BF16).reshape(frames, rows, width, chans)


def local(latents, clip_ids, gain_in, w_space, w_time, gain_attn, w_qkv, w_out):
    frames, rows, width, chans = latents.shape
    groups, count = lax.axis_size("rows"), lax.axis_size("tm")
    height = groups * rows
    spots = height * width
    shape = jax.ShapeDtypeStruct
    params = pltpu.CompilerParams(vmem_limit_bytes=(28 if frames * spots <= 1024 else 60) << 20)
    assert frames + 1 >= LONGEST

    if groups == 2:
        parts = [latents, lax.ppermute(latents, "rows", [(0, 1), (1, 0)])]
    else:
        everything = lax.all_gather(latents, "rows")
        parts = [everything[i] for i in range(groups)]

    shard = jnp.transpose(w_space, (0, 1, 3, 2))
    if shard.shape[2] % 16 == 0 and count % 8 == 0:
        found = gather_ring(shard, count)
        cut = len(found) // 2
    else:
        whole = lax.all_gather(shard, "tm", axis=2, tiled=True)
        half = chans // 2
        found = [(whole[:, :, :half], 0), (whole[:, :, half:], 1)]
        cut = 1
    shards = [pair[0] for pair in found]
    tags = [pair[1] for pair in found]
    split = cut * (chans // len(tags))

    wide, lat, head, tail = pl.pallas_call(
        functools.partial(prepare_kernel, tags),
        out_shape=(
            shape((frames, height + 2, width, 3 * chans), BF16),
            shape((frames, height, width, chans), BF16),
            shape((3, split, chans), BF16),
            shape((3, chans - split, chans), BF16),
        ),
        in_specs=[VMEM] * (len(parts) + 2),
        out_specs=(VMEM, VMEM, VMEM, VMEM),
        compiler_params=params,
        name="prepare",
    )(*parts, gain_in.reshape(1, chans), w_time)

    rest, packet = pl.pallas_call(
        early_kernel,
        out_shape=(shape((frames, spots, chans), F32), shape((3, spots, chans), F32)),
        in_specs=[VMEM, VMEM, SMEM, VMEM] + [VMEM] * cut,
        out_specs=(VMEM, VMEM),
        compiler_params=params,
        name="early",
    )(wide, lat, clip_ids, head, *shards[:cut])
    acts, packet = pl.pallas_call(
        late_kernel,
        out_shape=(shape((frames, spots, chans - split), BF16), shape((3, spots, chans), BF16)),
        in_specs=[VMEM, SMEM, VMEM, VMEM] + [VMEM] * (len(tags) - cut),
        out_specs=(VMEM, VMEM),
        compiler_params=params,
        name="late",
    )(wide, clip_ids, tail, packet, *shards[cut:])
    packet = lax.ppermute(packet, "tm", [(i, i + 1) for i in range(count - 1)])
    rest = pl.pallas_call(
        rest_kernel,
        out_shape=shape((frames, spots, chans), F32),
        in_specs=[VMEM, SMEM, VMEM, VMEM],
        out_specs=VMEM,
        compiler_params=params,
        name="rest",
    )(acts, clip_ids, tail, rest)
    return pl.pallas_call(
        attend_kernel,
        out_shape=shape((frames, rows, width, chans), BF16),
        in_specs=[VMEM, VMEM, SMEM, VMEM, VMEM, VMEM],
        out_specs=VMEM,
        scratch_shapes=[
            pltpu.VMEM((frames, height, width, chans), BF16),
            pltpu.VMEM((frames, height, width, chans), BF16),
        ],
        compiler_params=params,
        name="attend",
    )(rest, packet, clip_ids, gain_attn.reshape(1, chans), w_qkv, w_out)


def solution(mesh):
    placed = (P("tm", "rows", None, None), P(), P(), P(None, None, None, "tm"), P(), P(), P(), P())
    return jax.shard_map(
        local, mesh=mesh, in_specs=placed, out_specs=P("tm", "rows", None, None), check_vma=False
    )
```

```python
import functools

import jax
import jax.numpy as jnp
from jax import lax
from jax.experimental import pallas as pl
from jax.experimental.pallas import tpu as pltpu
from jax.sharding import PartitionSpec as P

LONGEST = 9
VMEM = pl.BlockSpec(memory_space=pltpu.VMEM)
SMEM = pl.BlockSpec(memory_space=pltpu.SMEM)
F32 = jnp.float32
BF16 = jnp.bfloat16


def dot(a, b):
    return jnp.dot(a, b, preferred_element_type=F32)


def dot_t(a, b):
    return lax.dot_general(a, b, (((1,), (1,)), ((), ())), preferred_element_type=F32)


def spot_of(device, count):
    z, y = device // 4, (device // 2) % 2
    return z + y * (count // 2 - 1 - 2 * z)


def device_at(spot, core, count):
    y = spot // (count // 4)
    return (spot + y * (count // 2 - 1 - 2 * spot)) * 4 + y * 2 + core


def ring_pairs(count):
    ring = count // 2
    pairs = []
    for spot in range(ring):
        pairs.append((device_at(spot, 0, count), device_at((spot + 1) % ring, 0, count)))
        pairs.append((device_at(spot, 1, count), device_at((spot - 1) % ring, 1, count)))
    return pairs


def ring_tags(count):
    tags = [(0, 0, 0), (0, 0, 1)]
    for step in range(1, count // 4 + 1):
        tags += [(step, 0, 0), (step, 1, 1)]
        if step < count // 4:
            tags += [(step, 0, 1), (step, 1, 0)]
    return tags


def gather_ring(own, count, gates):
    ring = ring_pairs(count)
    cores = [(i, i ^ 1) for i in range(count)]
    last = count // 4
    twin = lax.ppermute(own, "tm", cores)
    found = [own, twin]
    streams = [own, twin]
    for step in range(1, last + 1):
        for stream in range(2 if step < last else 1):
            gate = gates.get((stream, step))
            if gate is not None:
                streams[stream] = lax.optimization_barrier((streams[stream], gate(found)))[0]
            streams[stream] = lax.ppermute(streams[stream], "tm", ring)
            found.append(streams[stream])
            found.append(lax.ppermute(streams[stream], "tm", cores))
    return found


def shard_owner(tag, device, count):
    step, swapped, flip = tag
    core = device % 2
    ring = count // 2
    away = (1 - 2 * core) * ((1 - 2 * swapped) * step)
    spot = (spot_of(device, count) - away + ring) % ring
    return device_at(spot, (core + flip) % 2, count)


def prepare_kernel(*refs):
    *parts, gain_ref, wide_ref, lat_ref = refs
    frames, rows, width, chans = parts[0].shape
    groups = len(parts)
    mine = lax.axis_index("rows")
    gain = gain_ref[...]
    column = lax.broadcasted_iota(jnp.int32, (rows * width, 1), 0) % width
    edge = jnp.zeros((width, 3 * chans), BF16)
    for frame in range(frames):
        wide_ref[frame, 0] = edge
        wide_ref[frame, groups * rows + 1] = edge
    for at, part in enumerate(parts):
        first = at * rows
        if groups == 2:
            first = (mine if at == 0 else 1 - mine) * rows
        for frame in range(frames):
            raw = part[frame]
            lat_ref[frame, pl.ds(first, rows)] = raw
            x = raw.reshape(rows * width, chans).astype(F32)
            y = x * lax.rsqrt(jnp.mean(x * x, axis=-1, keepdims=True) + 1e-06) * gain
            before = jnp.where(column == 0, 0.0, pltpu.roll(y, 1, 0))
            after = jnp.where(column == width - 1, 0.0, pltpu.roll(y, rows * width - 1, 0))
            for dx, v in enumerate((before, y, after)):
                wide_ref[frame, pl.ds(first + 1, rows), :, dx * chans : (dx + 1) * chans] = v.astype(
                    BF16
                ).reshape(rows, width, chans)


def order_kernel(tags, time_ref, head_ref, tail_ref):
    block = time_ref.shape[1] // len(tags)
    device = lax.axis_index("tm")
    for slot, tag in enumerate(tags):
        owner = tag
        if isinstance(tag, tuple):
            owner = shard_owner(tag, device, len(tags))
        source = pl.ds(pl.multiple_of(owner * block, block), block)
        to_ref, at = head_ref, slot * block
        if at >= head_ref.shape[1]:
            to_ref, at = tail_ref, at - head_ref.shape[1]
        for back in range(3):
            to_ref[back, at : at + block] = time_ref[back, source]


def convolve(wide_ref, shards):
    frames, height, width, wide = wide_ref.shape
    height -= 2
    total = None
    for dy in range(3):
        weights = jnp.concatenate(
            [jnp.concatenate([shard[dy, dx] for dx in range(3)], axis=-1) for shard in shards], axis=0
        )
        lhs = wide_ref[:, dy : dy + height].reshape(frames * height * width, wide)
        part = dot_t(lhs, weights)
        total = part if total is None else total + part
    acts = (total * jax.nn.sigmoid(total)).astype(BF16)
    return acts.reshape(frames, height * width, -1)


def keep(flag, values):
    return jnp.where(flag, values, jnp.zeros_like(values))


def temporal(acts, clips, weights, frames):
    first = lax.axis_index("tm") * frames
    spots, width = acts[0].shape
    lines = []
    for t in range(frames):
        line = [acts[t]]
        for back in (1, 2):
            if t < back:
                line.append(jnp.zeros((spots, width), BF16))
            else:
                line.append(keep(clips[first + t - back] == clips[first + t], acts[t - back]))
        lines.append(jnp.concatenate(line, axis=-1))
    lhs = jnp.concatenate(lines, axis=0)
    rhs = jnp.concatenate([weights[k] for k in range(3)], axis=0)
    return dot(lhs, rhs)


def packet_sums(acts, clips, weights, frames, lat=None):
    first = lax.axis_index("tm") * frames
    end = clips.shape[0] - 1
    next0 = clips[jnp.minimum(first + frames, end)]
    next1 = clips[jnp.minimum(first + frames + 1, end)]
    spots, width = acts[0].shape
    sums = [jnp.zeros((spots, width), F32) for _ in range(3)]
    base = None if lat is None else jnp.zeros(lat[0].shape, F32)
    for t in range(frames):
        inside = clips[first + t] == next0
        if lat is not None:
            base = base + keep(inside, lat[t].astype(F32))
        for back in range(min(3, t + 1)):
            both = jnp.logical_and(inside, clips[first + t - back] == next0)
            sums[back] = sums[back] + keep(both, acts[t - back].astype(F32))
    sums = [s.astype(BF16) for s in sums]
    last0 = keep(clips[first + frames - 1] == next0, acts[frames - 1])
    prev0 = keep(clips[first + frames - 2] == next0, acts[frames - 2])
    last1 = keep(clips[first + frames - 1] == next1, acts[frames - 1])
    by0 = dot(sums[0], weights[0])
    by1 = dot(jnp.concatenate([last0, sums[1]], axis=0), weights[1])
    by2 = dot(jnp.concatenate([prev0, last1, sums[2]], axis=0), weights[2])
    total = by0 + by1[spots:] + by2[2 * spots :]
    if base is not None:
        total = total + base
    return by1[:spots] + by2[:spots], by2[spots : 2 * spots], total


def early_kernel(wide_ref, *refs):
    *shards, acts_ref = refs
    acts_ref[...] = convolve(wide_ref, shards)


def first_kernel(lat0_ref, lat1_ref, acts0_ref, acts1_ref, clips, weights, rest_ref, packet_ref):
    acts = [ref[t] for ref in (acts0_ref, acts1_ref) for t in range(ref.shape[0])]
    lat = [ref[t].reshape(acts[0].shape[0], -1) for ref in (lat0_ref, lat1_ref) for t in range(ref.shape[0])]
    frames = len(acts)
    for i, part in enumerate(packet_sums(acts, clips, weights, frames, lat)):
        packet_ref[i] = part
    rest = temporal(acts, clips, weights, frames).reshape(rest_ref.shape)
    for t in range(frames):
        rest_ref[t] = rest[t] + lat[t].astype(F32)


def late_kernel(wide0_ref, wide1_ref, clips, weights, early_ref, *refs):
    *shards, acts_ref, packet_ref = refs
    half, frames = wide0_ref.shape[0], acts_ref.shape[0]
    acts_ref[:half] = convolve(wide0_ref, shards)
    acts_ref[half:] = convolve(wide1_ref, shards)
    acts = [acts_ref[t] for t in range(frames)]
    for i, part in enumerate(packet_sums(acts, clips, weights, frames)):
        packet_ref[i] = (early_ref[i] + part).astype(BF16)


def rest_kernel(acts_ref, clips, weights, early_ref, rest_ref):
    frames = acts_ref.shape[0]
    part = temporal([acts_ref[t] for t in range(frames)], clips, weights, frames)
    rest_ref[...] = early_ref[...] + part.reshape(rest_ref.shape)


def attend_kernel(rest_ref, packet_ref, clips, gain_ref, qkv_ref, proj_ref, out_ref, mixed_ref, normed_ref):
    frames, rows, width, chans = out_ref.shape
    height = mixed_ref.shape[1]
    spots = height * width
    own = rows * width
    first = lax.axis_index("tm") * frames
    mine = pl.ds(lax.axis_index("rows") * rows, rows)
    gain = gain_ref[...]

    number = jnp.int32(1)
    for back in range(1, LONGEST):
        at = first - back
        hit = jnp.logical_and(at >= 0, clips[jnp.maximum(at, 0)] == clips[first])
        number = number + hit.astype(jnp.int32)
    running = packet_ref[2].astype(F32)
    for t in range(frames):
        resid = rest_ref[t]
        if t < 2:
            resid = resid + packet_ref[t].astype(F32)
        if t > 0:
            same = clips[first + t] == clips[first + t - 1]
            running = keep(same, running)
            number = jnp.where(same, number + 1, 1)
        running = running + resid
        mixed = (resid + running / jnp.full((1, chans), number.astype(F32))).astype(BF16)
        mixed_ref[t] = mixed.reshape(height, width, chans)
        x = mixed.astype(F32)
        y = x * lax.rsqrt(jnp.mean(x * x, axis=-1, keepdims=True) + 1e-06) * gain
        normed_ref[t] = y.astype(BF16).reshape(height, width, chans)

    query = dot(normed_ref[:, mine].reshape(frames * own, chans), qkv_ref[:, :chans]).astype(BF16)
    both = dot(normed_ref[...].reshape(frames * spots, chans), qkv_ref[:, chans:]).astype(BF16)
    attended = []
    for t in range(frames):
        key = both[t * spots : (t + 1) * spots, :chans]
        value = both[t * spots : (t + 1) * spots, chans:]
        scores = dot_t(query[t * own : (t + 1) * own], key) * chans ** (-0.5)
        weights = jnp.exp(scores - jnp.max(scores, axis=-1, keepdims=True))
        probs = (weights / jnp.sum(weights, axis=-1, keepdims=True)).astype(BF16)
        attended.append(dot(probs, value).astype(BF16))
    result = dot(jnp.concatenate(attended, axis=0), proj_ref[...])
    result = result + mixed_ref[:, mine].reshape(frames * own, chans).astype(F32)
    out_ref[...] = result.astype(BF16).reshape(frames, rows, width, chans)


def local(latents, clip_ids, gain_in, w_space, w_time, gain_attn, w_qkv, w_out):
    frames, rows, width, chans = latents.shape
    groups, count = lax.axis_size("rows"), lax.axis_size("tm")
    height = groups * rows
    spots = height * width
    shape = jax.ShapeDtypeStruct
    params = pltpu.CompilerParams(vmem_limit_bytes=(28 if frames * spots <= 1024 else 60) << 20)
    assert frames + 1 >= LONGEST

    half = frames // 2
    halves = [latents[:half], latents[half:]]
    if groups == 2:
        swap = [(0, 1), (1, 0)]
        others = [lax.ppermute(part, "rows", swap) for part in halves]
        parts = [[own, other] for own, other in zip(halves, others)]
    else:
        everything = [lax.all_gather(part, "rows") for part in halves]
        parts = [[part[i] for i in range(groups)] for part in everything]

    shard = jnp.transpose(w_space, (0, 1, 3, 2))
    ringed = shard.shape[2] % 16 == 0 and count % 8 == 0
    tags = ring_tags(count) if ringed else [0, 1]
    cut = len(tags) // 2
    split = cut * (chans // len(tags))

    gain = gain_in.reshape(1, chans)
    prepared = [
        pl.pallas_call(
            prepare_kernel,
            out_shape=(
                shape((half, height + 2, width, 3 * chans), BF16),
                shape((half, height, width, chans), BF16),
            ),
            in_specs=[VMEM] * (groups + 1),
            out_specs=(VMEM, VMEM),
            compiler_params=params,
            name="prepare",
        )(*part, gain)
        for part in parts
    ]
    wides = [pair[0] for pair in prepared]
    lats = [pair[1] for pair in prepared]
    head, tail = pl.pallas_call(
        functools.partial(order_kernel, tags),
        out_shape=(shape((3, split, chans), BF16), shape((3, chans - split, chans), BF16)),
        in_specs=[VMEM],
        out_specs=(VMEM, VMEM),
        compiler_params=params,
        name="order",
    )(w_time)

    acts = [None, None]

    def early(which, shards):
        acts[which] = pl.pallas_call(
            early_kernel,
            out_shape=shape((half, spots, split), BF16),
            in_specs=[VMEM] * (1 + cut),
            out_specs=VMEM,
            compiler_params=params,
            name="early",
        )(wides[which], *shards[:cut])
        return acts[which]

    if ringed:
        last = count // 4
        gates = {
            (1, 2): lambda found: parts[0][1],
            (0, last - 1): lambda found: parts[1][1],
            (1, last - 1): functools.partial(early, 0),
            (0, last): functools.partial(early, 1),
        }
        shards = gather_ring(shard, count, gates)
    else:
        whole = lax.all_gather(shard, "tm", axis=2, tiled=True)
        shards = [whole[:, :, :split], whole[:, :, split:]]
        early(0, shards)
        early(1, shards)

    rest, packet = pl.pallas_call(
        first_kernel,
        out_shape=(shape((frames, spots, chans), F32), shape((3, spots, chans), F32)),
        in_specs=[VMEM] * 4 + [SMEM, VMEM],
        out_specs=(VMEM, VMEM),
        compiler_params=params,
        name="first",
    )(*lats, *acts, clip_ids, head)
    acts, packet = pl.pallas_call(
        late_kernel,
        out_shape=(shape((frames, spots, chans - split), BF16), shape((3, spots, chans), BF16)),
        in_specs=[VMEM, VMEM, SMEM, VMEM, VMEM] + [VMEM] * (len(tags) - cut),
        out_specs=(VMEM, VMEM),
        compiler_params=params,
        name="late",
    )(*wides, clip_ids, tail, packet, *shards[cut:])
    packet = lax.ppermute(packet, "tm", [(i, i + 1) for i in range(count - 1)])
    rest = pl.pallas_call(
        rest_kernel,
        out_shape=shape((frames, spots, chans), F32),
        in_specs=[VMEM, SMEM, VMEM, VMEM],
        out_specs=VMEM,
        compiler_params=params,
        name="rest",
    )(acts, clip_ids, tail, rest)
    return pl.pallas_call(
        attend_kernel,
        out_shape=shape((frames, rows, width, chans), BF16),
        in_specs=[VMEM, VMEM, SMEM, VMEM, VMEM, VMEM],
        out_specs=VMEM,
        scratch_shapes=[
            pltpu.VMEM((frames, height, width, chans), BF16),
            pltpu.VMEM((frames, height, width, chans), BF16),
        ],
        compiler_params=params,
        name="attend",
    )(rest, packet, clip_ids, gain_attn.reshape(1, chans), w_qkv, w_out)


def solution(mesh):
    placed = (P("tm", "rows", None, None), P(), P(), P(None, None, None, "tm"), P(), P(), P(), P())
    return jax.shard_map(
        local, mesh=mesh, in_specs=placed, out_specs=P("tm", "rows", None, None), check_vma=False
    )
```

```python
import functools

import jax
import jax.numpy as jnp
from jax import lax
from jax.experimental import pallas as pl
from jax.experimental.pallas import tpu as pltpu
from jax.sharding import PartitionSpec as P

LONGEST = 9
VMEM = pl.BlockSpec(memory_space=pltpu.VMEM)
SMEM = pl.BlockSpec(memory_space=pltpu.SMEM)
F32 = jnp.float32
BF16 = jnp.bfloat16


def dot(a, b):
    return jnp.dot(a, b, preferred_element_type=F32)


def dot_t(a, b):
    return lax.dot_general(a, b, (((1,), (1,)), ((), ())), preferred_element_type=F32)


def spot_of(device, count):
    z, y = device // 4, (device // 2) % 2
    return z + y * (count // 2 - 1 - 2 * z)


def device_at(spot, core, count):
    y = spot // (count // 4)
    return (spot + y * (count // 2 - 1 - 2 * spot)) * 4 + y * 2 + core


def ring_pairs(count):
    ring = count // 2
    pairs = []
    for spot in range(ring):
        pairs.append((device_at(spot, 0, count), device_at((spot + 1) % ring, 0, count)))
        pairs.append((device_at(spot, 1, count), device_at((spot - 1) % ring, 1, count)))
    return pairs


def ring_tags(count):
    tags = [(0, 0, 0), (0, 0, 1)]
    for step in range(1, count // 4 + 1):
        tags += [(step, 0, 0), (step, 1, 1)]
        if step < count // 4:
            tags += [(step, 0, 1), (step, 1, 0)]
    return tags


def gather_ring(own, count, gates):
    ring = ring_pairs(count)
    cores = [(i, i ^ 1) for i in range(count)]
    last = count // 4
    found = [own, lax.ppermute(own, "tm", cores)]
    streams = [own, own]
    for step in range(1, last + 1):
        for stream in range(2 if step < last else 1):
            gate = gates.get((stream, step))
            if gate is not None:
                streams[stream] = lax.optimization_barrier((streams[stream], gate(found)))[0]
            pairs = ring
            if stream == 1 and step == 1:
                pairs = [(source ^ 1, target) for source, target in ring]
            streams[stream] = lax.ppermute(streams[stream], "tm", pairs)
            found.append(streams[stream])
            found.append(lax.ppermute(streams[stream], "tm", cores))
    return found


def shard_owner(tag, device, count):
    step, swapped, flip = tag
    core = device % 2
    ring = count // 2
    away = (1 - 2 * core) * ((1 - 2 * swapped) * step)
    spot = (spot_of(device, count) - away + ring) % ring
    return device_at(spot, (core + flip) % 2, count)


def prepare_kernel(*refs):
    *parts, gain_ref, wide_ref, lat_ref = refs
    frames, rows, width, chans = parts[0].shape
    groups = len(parts)
    mine = lax.axis_index("rows")
    gain = gain_ref[...]
    column = lax.broadcasted_iota(jnp.int32, (rows * width, 1), 0) % width
    edge = jnp.zeros((width, 3 * chans), BF16)
    for frame in range(frames):
        wide_ref[frame, 0] = edge
        wide_ref[frame, groups * rows + 1] = edge
    for at, part in enumerate(parts):
        first = at * rows
        if groups == 2:
            first = (mine if at == 0 else 1 - mine) * rows
        for frame in range(frames):
            raw = part[frame]
            lat_ref[frame, pl.ds(first, rows)] = raw
            x = raw.reshape(rows * width, chans).astype(F32)
            y = x * lax.rsqrt(jnp.mean(x * x, axis=-1, keepdims=True) + 1e-06) * gain
            before = jnp.where(column == 0, 0.0, pltpu.roll(y, 1, 0))
            after = jnp.where(column == width - 1, 0.0, pltpu.roll(y, rows * width - 1, 0))
            for dx, v in enumerate((before, y, after)):
                wide_ref[frame, pl.ds(first + 1, rows), :, dx * chans : (dx + 1) * chans] = v.astype(
                    BF16
                ).reshape(rows, width, chans)


def order_kernel(tags, time_ref, head_ref, tail_ref):
    block = time_ref.shape[1] // len(tags)
    device = lax.axis_index("tm")
    for slot, tag in enumerate(tags):
        owner = tag
        if isinstance(tag, tuple):
            owner = shard_owner(tag, device, len(tags))
        source = pl.ds(pl.multiple_of(owner * block, block), block)
        to_ref, at = head_ref, slot * block
        if at >= head_ref.shape[1]:
            to_ref, at = tail_ref, at - head_ref.shape[1]
        for back in range(3):
            to_ref[back, at : at + block] = time_ref[back, source]


def convolve(wide_ref, shards):
    frames, height, width, wide = wide_ref.shape
    height -= 2
    total = None
    for dy in range(3):
        weights = jnp.concatenate(
            [jnp.concatenate([shard[dy, dx] for dx in range(3)], axis=-1) for shard in shards], axis=0
        )
        lhs = wide_ref[:, dy : dy + height].reshape(frames * height * width, wide)
        part = dot_t(lhs, weights)
        total = part if total is None else total + part
    acts = (total * jax.nn.sigmoid(total)).astype(BF16)
    return acts.reshape(frames, height * width, -1)


def keep(flag, values):
    return jnp.where(flag, values, jnp.zeros_like(values))


def temporal(acts, clips, weights, frames):
    first = lax.axis_index("tm") * frames
    spots, width = acts[0].shape
    lines = []
    for t in range(frames):
        line = [acts[t]]
        for back in (1, 2):
            if t < back:
                line.append(jnp.zeros((spots, width), BF16))
            else:
                line.append(keep(clips[first + t - back] == clips[first + t], acts[t - back]))
        lines.append(jnp.concatenate(line, axis=-1))
    lhs = jnp.concatenate(lines, axis=0)
    rhs = jnp.concatenate([weights[k] for k in range(3)], axis=0)
    return dot(lhs, rhs)


def packet_sums(acts, clips, weights, frames, lat=None):
    first = lax.axis_index("tm") * frames
    end = clips.shape[0] - 1
    next0 = clips[jnp.minimum(first + frames, end)]
    next1 = clips[jnp.minimum(first + frames + 1, end)]
    spots, width = acts[0].shape
    sums = [jnp.zeros((spots, width), F32) for _ in range(3)]
    base = None if lat is None else jnp.zeros(lat[0].shape, F32)
    for t in range(frames):
        inside = clips[first + t] == next0
        if lat is not None:
            base = base + keep(inside, lat[t].astype(F32))
        for back in range(min(3, t + 1)):
            both = jnp.logical_and(inside, clips[first + t - back] == next0)
            sums[back] = sums[back] + keep(both, acts[t - back].astype(F32))
    sums = [s.astype(BF16) for s in sums]
    last0 = keep(clips[first + frames - 1] == next0, acts[frames - 1])
    prev0 = keep(clips[first + frames - 2] == next0, acts[frames - 2])
    last1 = keep(clips[first + frames - 1] == next1, acts[frames - 1])
    by0 = dot(sums[0], weights[0])
    by1 = dot(jnp.concatenate([last0, sums[1]], axis=0), weights[1])
    by2 = dot(jnp.concatenate([prev0, last1, sums[2]], axis=0), weights[2])
    total = by0 + by1[spots:] + by2[2 * spots :]
    if base is not None:
        total = total + base
    return by1[:spots] + by2[:spots], by2[spots : 2 * spots], total


def early_kernel(wide_ref, *refs):
    *shards, acts_ref = refs
    acts_ref[...] = convolve(wide_ref, shards)


def first_kernel(lat0_ref, lat1_ref, acts0_ref, acts1_ref, clips, weights, rest_ref, packet_ref):
    acts = [ref[t] for ref in (acts0_ref, acts1_ref) for t in range(ref.shape[0])]
    lat = [ref[t].reshape(acts[0].shape[0], -1) for ref in (lat0_ref, lat1_ref) for t in range(ref.shape[0])]
    frames = len(acts)
    for i, part in enumerate(packet_sums(acts, clips, weights, frames, lat)):
        packet_ref[i] = part
    rest = temporal(acts, clips, weights, frames).reshape(rest_ref.shape)
    for t in range(frames):
        rest_ref[t] = rest[t] + lat[t].astype(F32)


def late_kernel(wide0_ref, wide1_ref, clips, weights, early_ref, *refs):
    *shards, acts_ref, packet_ref = refs
    half, frames = wide0_ref.shape[0], acts_ref.shape[0]
    acts_ref[:half] = convolve(wide0_ref, shards)
    acts_ref[half:] = convolve(wide1_ref, shards)
    acts = [acts_ref[t] for t in range(frames)]
    for i, part in enumerate(packet_sums(acts, clips, weights, frames)):
        packet_ref[i] = (early_ref[i] + part).astype(BF16)


def rest_kernel(acts_ref, clips, weights, early_ref, rest_ref):
    frames = acts_ref.shape[0]
    part = temporal([acts_ref[t] for t in range(frames)], clips, weights, frames)
    rest_ref[...] = early_ref[...] + part.reshape(rest_ref.shape)


def attend_kernel(rest_ref, packet_ref, clips, gain_ref, qkv_ref, proj_ref, out_ref, mixed_ref, normed_ref):
    frames, rows, width, chans = out_ref.shape
    height = mixed_ref.shape[1]
    spots = height * width
    own = rows * width
    first = lax.axis_index("tm") * frames
    mine = pl.ds(lax.axis_index("rows") * rows, rows)
    gain = gain_ref[...]

    number = jnp.int32(1)
    for back in range(1, LONGEST):
        at = first - back
        hit = jnp.logical_and(at >= 0, clips[jnp.maximum(at, 0)] == clips[first])
        number = number + hit.astype(jnp.int32)
    running = packet_ref[2].astype(F32)
    for t in range(frames):
        resid = rest_ref[t]
        if t < 2:
            resid = resid + packet_ref[t].astype(F32)
        if t > 0:
            same = clips[first + t] == clips[first + t - 1]
            running = keep(same, running)
            number = jnp.where(same, number + 1, 1)
        running = running + resid
        mixed = (resid + running / jnp.full((1, chans), number.astype(F32))).astype(BF16)
        mixed_ref[t] = mixed.reshape(height, width, chans)
        x = mixed.astype(F32)
        y = x * lax.rsqrt(jnp.mean(x * x, axis=-1, keepdims=True) + 1e-06) * gain
        normed_ref[t] = y.astype(BF16).reshape(height, width, chans)

    query = dot(normed_ref[:, mine].reshape(frames * own, chans), qkv_ref[:, :chans]).astype(BF16)
    both = dot(normed_ref[...].reshape(frames * spots, chans), qkv_ref[:, chans:]).astype(BF16)
    attended = []
    for t in range(frames):
        key = both[t * spots : (t + 1) * spots, :chans]
        value = both[t * spots : (t + 1) * spots, chans:]
        scores = dot_t(query[t * own : (t + 1) * own], key) * chans ** (-0.5)
        weights = jnp.exp(scores - jnp.max(scores, axis=-1, keepdims=True))
        probs = (weights / jnp.sum(weights, axis=-1, keepdims=True)).astype(BF16)
        attended.append(dot(probs, value).astype(BF16))
    result = dot(jnp.concatenate(attended, axis=0), proj_ref[...])
    result = result + mixed_ref[:, mine].reshape(frames * own, chans).astype(F32)
    out_ref[...] = result.astype(BF16).reshape(frames, rows, width, chans)


def local(latents, clip_ids, gain_in, w_space, w_time, gain_attn, w_qkv, w_out):
    frames, rows, width, chans = latents.shape
    groups, count = lax.axis_size("rows"), lax.axis_size("tm")
    height = groups * rows
    spots = height * width
    shape = jax.ShapeDtypeStruct
    params = pltpu.CompilerParams(vmem_limit_bytes=(28 if frames * spots <= 1024 else 60) << 20)
    assert frames + 1 >= LONGEST

    half = frames // 2 + 1
    halves = [latents[:half], latents[half:]]
    if groups == 2:
        swap = [(0, 1), (1, 0)]
        others = [lax.ppermute(part, "rows", swap) for part in halves]
        parts = [[own, other] for own, other in zip(halves, others)]
    else:
        everything = [lax.all_gather(part, "rows") for part in halves]
        parts = [[part[i] for i in range(groups)] for part in everything]

    shard = jnp.transpose(w_space, (0, 1, 3, 2))
    ringed = shard.shape[2] % 16 == 0 and count % 8 == 0
    tags = ring_tags(count) if ringed else [0, 1]
    cut = len(tags) // 2
    split = cut * (chans // len(tags))

    gain = gain_in.reshape(1, chans)
    prepared = [
        pl.pallas_call(
            prepare_kernel,
            out_shape=(
                shape((part[0].shape[0], height + 2, width, 3 * chans), BF16),
                shape((part[0].shape[0], height, width, chans), BF16),
            ),
            in_specs=[VMEM] * (groups + 1),
            out_specs=(VMEM, VMEM),
            compiler_params=params,
            name="prepare",
        )(*part, gain)
        for part in parts
    ]
    wides = [pair[0] for pair in prepared]
    lats = [pair[1] for pair in prepared]
    head, tail = pl.pallas_call(
        functools.partial(order_kernel, tags),
        out_shape=(shape((3, split, chans), BF16), shape((3, chans - split, chans), BF16)),
        in_specs=[VMEM],
        out_specs=(VMEM, VMEM),
        compiler_params=params,
        name="order",
    )(w_time)

    acts = [None, None]

    def early(which, shards):
        acts[which] = pl.pallas_call(
            early_kernel,
            out_shape=shape((wides[which].shape[0], spots, split), BF16),
            in_specs=[VMEM] * (1 + cut),
            out_specs=VMEM,
            compiler_params=params,
            name="early",
        )(wides[which], *shards[:cut])
        return acts[which]

    if ringed:
        last = count // 4
        gates = {
            (0, 2): lambda found: parts[0][1],
            (0, last - 1): lambda found: parts[1][1],
            (1, last - 1): functools.partial(early, 0),
            (0, last): functools.partial(early, 1),
        }
        shards = gather_ring(shard, count, gates)
    else:
        whole = lax.all_gather(shard, "tm", axis=2, tiled=True)
        shards = [whole[:, :, :split], whole[:, :, split:]]
        early(0, shards)
        early(1, shards)

    rest, packet = pl.pallas_call(
        first_kernel,
        out_shape=(shape((frames, spots, chans), F32), shape((3, spots, chans), F32)),
        in_specs=[VMEM] * 4 + [SMEM, VMEM],
        out_specs=(VMEM, VMEM),
        compiler_params=params,
        name="first",
    )(*lats, *acts, clip_ids, head)
    acts, packet = pl.pallas_call(
        late_kernel,
        out_shape=(shape((frames, spots, chans - split), BF16), shape((3, spots, chans), BF16)),
        in_specs=[VMEM, VMEM, SMEM, VMEM, VMEM] + [VMEM] * (len(tags) - cut),
        out_specs=(VMEM, VMEM),
        compiler_params=params,
        name="late",
    )(*wides, clip_ids, tail, packet, *shards[cut:])
    packet = lax.ppermute(packet, "tm", [(i, i + 1) for i in range(count - 1)])
    rest = pl.pallas_call(
        rest_kernel,
        out_shape=shape((frames, spots, chans), F32),
        in_specs=[VMEM, SMEM, VMEM, VMEM],
        out_specs=VMEM,
        compiler_params=params,
        name="rest",
    )(acts, clip_ids, tail, rest)
    return pl.pallas_call(
        attend_kernel,
        out_shape=shape((frames, rows, width, chans), BF16),
        in_specs=[VMEM, VMEM, SMEM, VMEM, VMEM, VMEM],
        out_specs=VMEM,
        scratch_shapes=[
            pltpu.VMEM((frames, height, width, chans), BF16),
            pltpu.VMEM((frames, height, width, chans), BF16),
        ],
        compiler_params=params,
        name="attend",
    )(rest, packet, clip_ids, gain_attn.reshape(1, chans), w_qkv, w_out)


def solution(mesh):
    placed = (P("tm", "rows", None, None), P(), P(), P(None, None, None, "tm"), P(), P(), P(), P())
    return jax.shard_map(
        local, mesh=mesh, in_specs=placed, out_specs=P("tm", "rows", None, None), check_vma=False
    )
```

```python
import functools

import jax
import jax.numpy as jnp
from jax import lax
from jax.experimental import pallas as pl
from jax.experimental.pallas import tpu as pltpu
from jax.sharding import PartitionSpec as P

LONGEST = 9
VMEM = pl.BlockSpec(memory_space=pltpu.VMEM)
SMEM = pl.BlockSpec(memory_space=pltpu.SMEM)
F32 = jnp.float32
BF16 = jnp.bfloat16


def dot(a, b):
    return jnp.dot(a, b, preferred_element_type=F32)


def dot_t(a, b):
    return lax.dot_general(a, b, (((1,), (1,)), ((), ())), preferred_element_type=F32)


def spot_of(device, count):
    z, y = device // 4, (device // 2) % 2
    return z + y * (count // 2 - 1 - 2 * z)


def device_at(spot, core, count):
    y = spot // (count // 4)
    return (spot + y * (count // 2 - 1 - 2 * spot)) * 4 + y * 2 + core


def ring_pairs(count):
    ring = count // 2
    pairs = []
    for spot in range(ring):
        pairs.append((device_at(spot, 0, count), device_at((spot + 1) % ring, 0, count)))
        pairs.append((device_at(spot, 1, count), device_at((spot - 1) % ring, 1, count)))
    return pairs


def ring_tags(count):
    tags = [(0, 0, 0), (0, 0, 1)]
    for step in range(1, count // 4 + 1):
        tags += [(step, 0, 0), (step, 1, 1)]
        if step < count // 4:
            tags += [(step, 0, 1), (step, 1, 0)]
    return tags


def gather_ring(own, count, gates):
    ring = ring_pairs(count)
    cores = [(i, i ^ 1) for i in range(count)]
    last = count // 4
    found = [own, lax.ppermute(own, "tm", cores)]
    streams = list(found)
    for step in range(1, last + 1):
        for stream in range(2 if step < last else 1):
            gate = gates.get((stream, step))
            if gate is not None:
                streams[stream] = lax.optimization_barrier((streams[stream], gate(found)))[0]
            streams[stream] = lax.ppermute(streams[stream], "tm", ring)
            found.append(streams[stream])
            found.append(lax.ppermute(streams[stream], "tm", cores))
    return found


def shard_owner(tag, device, count):
    step, swapped, flip = tag
    core = device % 2
    ring = count // 2
    away = (1 - 2 * core) * ((1 - 2 * swapped) * step)
    spot = (spot_of(device, count) - away + ring) % ring
    return device_at(spot, (core + flip) % 2, count)


def prepare_kernel(start, *refs):
    *parts, gain_ref, wide_ref, lat_ref = refs
    _, rows, width, chans = parts[0].shape
    frames = wide_ref.shape[0]
    groups = len(parts)
    mine = lax.axis_index("rows")
    gain = gain_ref[...]
    column = lax.broadcasted_iota(jnp.int32, (rows * width, 1), 0) % width
    edge = jnp.zeros((width, 3 * chans), BF16)
    for frame in range(frames):
        wide_ref[frame, 0] = edge
        wide_ref[frame, groups * rows + 1] = edge
    for at, part in enumerate(parts):
        first = at * rows
        if groups == 2:
            first = (mine if at == 0 else 1 - mine) * rows
        for frame in range(frames):
            raw = part[start + frame]
            lat_ref[frame, pl.ds(first, rows)] = raw
            x = raw.reshape(rows * width, chans).astype(F32)
            y = x * lax.rsqrt(jnp.mean(x * x, axis=-1, keepdims=True) + 1e-06) * gain
            before = jnp.where(column == 0, 0.0, pltpu.roll(y, 1, 0))
            after = jnp.where(column == width - 1, 0.0, pltpu.roll(y, rows * width - 1, 0))
            for dx, v in enumerate((before, y, after)):
                wide_ref[frame, pl.ds(first + 1, rows), :, dx * chans : (dx + 1) * chans] = v.astype(
                    BF16
                ).reshape(rows, width, chans)


def order_kernel(tags, time_ref, head_ref, tail_ref):
    block = time_ref.shape[1] // len(tags)
    device = lax.axis_index("tm")
    for slot, tag in enumerate(tags):
        owner = tag
        if isinstance(tag, tuple):
            owner = shard_owner(tag, device, len(tags))
        source = pl.ds(pl.multiple_of(owner * block, block), block)
        to_ref, at = head_ref, slot * block
        if at >= head_ref.shape[1]:
            to_ref, at = tail_ref, at - head_ref.shape[1]
        for back in range(3):
            to_ref[back, at : at + block] = time_ref[back, source]


def convolve(wide_ref, shards):
    frames, height, width, wide = wide_ref.shape
    height -= 2
    total = None
    for dy in range(3):
        weights = jnp.concatenate(
            [jnp.concatenate([shard[dy, dx] for dx in range(3)], axis=-1) for shard in shards], axis=0
        )
        lhs = wide_ref[:, dy : dy + height].reshape(frames * height * width, wide)
        part = dot_t(lhs, weights)
        total = part if total is None else total + part
    acts = (total * jax.nn.sigmoid(total)).astype(BF16)
    return acts.reshape(frames, height * width, -1)


def keep(flag, values):
    return jnp.where(flag, values, jnp.zeros_like(values))


def temporal(acts, clips, weights, frames):
    first = lax.axis_index("tm") * frames
    spots, width = acts[0].shape
    lines = []
    for t in range(frames):
        line = [acts[t]]
        for back in (1, 2):
            if t < back:
                line.append(jnp.zeros((spots, width), BF16))
            else:
                line.append(keep(clips[first + t - back] == clips[first + t], acts[t - back]))
        lines.append(jnp.concatenate(line, axis=-1))
    lhs = jnp.concatenate(lines, axis=0)
    rhs = jnp.concatenate([weights[k] for k in range(3)], axis=0)
    return dot(lhs, rhs)


def packet_sums(acts, clips, weights, frames, lat=None):
    first = lax.axis_index("tm") * frames
    end = clips.shape[0] - 1
    next0 = clips[jnp.minimum(first + frames, end)]
    next1 = clips[jnp.minimum(first + frames + 1, end)]
    spots, width = acts[0].shape
    sums = [jnp.zeros((spots, width), F32) for _ in range(3)]
    base = None if lat is None else jnp.zeros(lat[0].shape, F32)
    for t in range(frames):
        inside = clips[first + t] == next0
        if lat is not None:
            base = base + keep(inside, lat[t].astype(F32))
        for back in range(min(3, t + 1)):
            both = jnp.logical_and(inside, clips[first + t - back] == next0)
            sums[back] = sums[back] + keep(both, acts[t - back].astype(F32))
    sums = [s.astype(BF16) for s in sums]
    last0 = keep(clips[first + frames - 1] == next0, acts[frames - 1])
    prev0 = keep(clips[first + frames - 2] == next0, acts[frames - 2])
    last1 = keep(clips[first + frames - 1] == next1, acts[frames - 1])
    by0 = dot(sums[0], weights[0])
    by1 = dot(jnp.concatenate([last0, sums[1]], axis=0), weights[1])
    by2 = dot(jnp.concatenate([prev0, last1, sums[2]], axis=0), weights[2])
    total = by0 + by1[spots:] + by2[2 * spots :]
    if base is not None:
        total = total + base
    return by1[:spots] + by2[:spots], by2[spots : 2 * spots], total


def early_kernel(wide_ref, *refs):
    *shards, acts_ref = refs
    acts_ref[...] = convolve(wide_ref, shards)


def first_kernel(lat0_ref, lat1_ref, acts0_ref, acts1_ref, clips, weights, rest_ref, packet_ref):
    acts = [ref[t] for ref in (acts0_ref, acts1_ref) for t in range(ref.shape[0])]
    lat = [ref[t].reshape(acts[0].shape[0], -1) for ref in (lat0_ref, lat1_ref) for t in range(ref.shape[0])]
    frames = len(acts)
    for i, part in enumerate(packet_sums(acts, clips, weights, frames, lat)):
        packet_ref[i] = part
    rest = temporal(acts, clips, weights, frames).reshape(rest_ref.shape)
    for t in range(frames):
        rest_ref[t] = rest[t] + lat[t].astype(F32)


def late_kernel(wide0_ref, wide1_ref, clips, weights, early_ref, *refs):
    *shards, acts_ref, packet_ref = refs
    half, frames = wide0_ref.shape[0], acts_ref.shape[0]
    acts_ref[:half] = convolve(wide0_ref, shards)
    acts_ref[half:] = convolve(wide1_ref, shards)
    acts = [acts_ref[t] for t in range(frames)]
    for i, part in enumerate(packet_sums(acts, clips, weights, frames)):
        packet_ref[i] = (early_ref[i] + part).astype(BF16)


def rest_kernel(acts_ref, clips, weights, early_ref, rest_ref):
    frames = acts_ref.shape[0]
    part = temporal([acts_ref[t] for t in range(frames)], clips, weights, frames)
    rest_ref[...] = early_ref[...] + part.reshape(rest_ref.shape)


def attend_kernel(rest_ref, packet_ref, clips, gain_ref, qkv_ref, proj_ref, out_ref, mixed_ref, normed_ref):
    frames, rows, width, chans = out_ref.shape
    height = mixed_ref.shape[1]
    spots = height * width
    own = rows * width
    first = lax.axis_index("tm") * frames
    mine = pl.ds(lax.axis_index("rows") * rows, rows)
    gain = gain_ref[...]

    number = jnp.int32(1)
    for back in range(1, LONGEST):
        at = first - back
        hit = jnp.logical_and(at >= 0, clips[jnp.maximum(at, 0)] == clips[first])
        number = number + hit.astype(jnp.int32)
    running = packet_ref[2].astype(F32)
    for t in range(frames):
        resid = rest_ref[t]
        if t < 2:
            resid = resid + packet_ref[t].astype(F32)
        if t > 0:
            same = clips[first + t] == clips[first + t - 1]
            running = keep(same, running)
            number = jnp.where(same, number + 1, 1)
        running = running + resid
        mixed = (resid + running / jnp.full((1, chans), number.astype(F32))).astype(BF16)
        mixed_ref[t] = mixed.reshape(height, width, chans)
        x = mixed.astype(F32)
        y = x * lax.rsqrt(jnp.mean(x * x, axis=-1, keepdims=True) + 1e-06) * gain
        normed_ref[t] = y.astype(BF16).reshape(height, width, chans)

    query = dot(normed_ref[:, mine].reshape(frames * own, chans), qkv_ref[:, :chans]).astype(BF16)
    both = dot(normed_ref[...].reshape(frames * spots, chans), qkv_ref[:, chans:]).astype(BF16)
    attended = []
    for t in range(frames):
        key = both[t * spots : (t + 1) * spots, :chans]
        value = both[t * spots : (t + 1) * spots, chans:]
        scores = dot_t(query[t * own : (t + 1) * own], key) * chans ** (-0.5)
        weights = jnp.exp(scores - jnp.max(scores, axis=-1, keepdims=True))
        probs = (weights / jnp.sum(weights, axis=-1, keepdims=True)).astype(BF16)
        attended.append(dot(probs, value).astype(BF16))
    result = dot(jnp.concatenate(attended, axis=0), proj_ref[...])
    result = result + mixed_ref[:, mine].reshape(frames * own, chans).astype(F32)
    out_ref[...] = result.astype(BF16).reshape(frames, rows, width, chans)


def local(latents, clip_ids, gain_in, w_space, w_time, gain_attn, w_qkv, w_out):
    frames, rows, width, chans = latents.shape
    groups, count = lax.axis_size("rows"), lax.axis_size("tm")
    height = groups * rows
    spots = height * width
    shape = jax.ShapeDtypeStruct
    params = pltpu.CompilerParams(vmem_limit_bytes=(28 if frames * spots <= 1024 else 60) << 20)
    assert frames + 1 >= LONGEST

    half = frames // 2
    if groups == 2:
        parts = [latents, lax.ppermute(latents, "rows", [(0, 1), (1, 0)])]
    else:
        everything = lax.all_gather(latents, "rows")
        parts = [everything[i] for i in range(groups)]

    shard = jnp.transpose(w_space, (0, 1, 3, 2))
    ringed = shard.shape[2] % 16 == 0 and count % 8 == 0
    tags = ring_tags(count) if ringed else [0, 1]
    cut = len(tags) // 2
    split = cut * (chans // len(tags))

    gain = gain_in.reshape(1, chans)
    prepared = [
        pl.pallas_call(
            functools.partial(prepare_kernel, start),
            out_shape=(
                shape((half, height + 2, width, 3 * chans), BF16),
                shape((half, height, width, chans), BF16),
            ),
            in_specs=[VMEM] * (groups + 1),
            out_specs=(VMEM, VMEM),
            compiler_params=params,
            name="prepare",
        )(*parts, gain)
        for start in (0, half)
    ]
    wides = [pair[0] for pair in prepared]
    lats = [pair[1] for pair in prepared]
    head, tail = pl.pallas_call(
        functools.partial(order_kernel, tags),
        out_shape=(shape((3, split, chans), BF16), shape((3, chans - split, chans), BF16)),
        in_specs=[VMEM],
        out_specs=(VMEM, VMEM),
        compiler_params=params,
        name="order",
    )(w_time)

    acts = [None, None]

    def early(which, shards):
        acts[which] = pl.pallas_call(
            early_kernel,
            out_shape=shape((wides[which].shape[0], spots, split), BF16),
            in_specs=[VMEM] * (1 + cut),
            out_specs=VMEM,
            compiler_params=params,
            name="early",
        )(wides[which], *shards[:cut])
        return acts[which]

    if ringed:
        last = count // 4
        gates = {
            (1, 2): lambda found: parts[1],
            (1, last - 1): functools.partial(early, 0),
            (0, last): functools.partial(early, 1),
        }
        shards = gather_ring(shard, count, gates)
    else:
        whole = lax.all_gather(shard, "tm", axis=2, tiled=True)
        shards = [whole[:, :, :split], whole[:, :, split:]]
        early(0, shards)
        early(1, shards)

    rest, packet = pl.pallas_call(
        first_kernel,
        out_shape=(shape((frames, spots, chans), F32), shape((3, spots, chans), F32)),
        in_specs=[VMEM] * 4 + [SMEM, VMEM],
        out_specs=(VMEM, VMEM),
        compiler_params=params,
        name="first",
    )(*lats, *acts, clip_ids, head)
    acts, packet = pl.pallas_call(
        late_kernel,
        out_shape=(shape((frames, spots, chans - split), BF16), shape((3, spots, chans), BF16)),
        in_specs=[VMEM, VMEM, SMEM, VMEM, VMEM] + [VMEM] * (len(tags) - cut),
        out_specs=(VMEM, VMEM),
        compiler_params=params,
        name="late",
    )(*wides, clip_ids, tail, packet, *shards[cut:])
    packet = lax.ppermute(packet, "tm", [(i, i + 1) for i in range(count - 1)])
    rest = pl.pallas_call(
        rest_kernel,
        out_shape=shape((frames, spots, chans), F32),
        in_specs=[VMEM, SMEM, VMEM, VMEM],
        out_specs=VMEM,
        compiler_params=params,
        name="rest",
    )(acts, clip_ids, tail, rest)
    return pl.pallas_call(
        attend_kernel,
        out_shape=shape((frames, rows, width, chans), BF16),
        in_specs=[VMEM, VMEM, SMEM, VMEM, VMEM, VMEM],
        out_specs=VMEM,
        scratch_shapes=[
            pltpu.VMEM((frames, height, width, chans), BF16),
            pltpu.VMEM((frames, height, width, chans), BF16),
        ],
        compiler_params=params,
        name="attend",
    )(rest, packet, clip_ids, gain_attn.reshape(1, chans), w_qkv, w_out)


def solution(mesh):
    placed = (P("tm", "rows", None, None), P(), P(), P(None, None, None, "tm"), P(), P(), P(), P())
    return jax.shard_map(
        local, mesh=mesh, in_specs=placed, out_specs=P("tm", "rows", None, None), check_vma=False
    )
```

```python
import functools

import jax
import jax.numpy as jnp
from jax import lax
from jax.experimental import pallas as pl
from jax.experimental.pallas import tpu as pltpu
from jax.sharding import PartitionSpec as P

LONGEST = 9
VMEM = pl.BlockSpec(memory_space=pltpu.VMEM)
SMEM = pl.BlockSpec(memory_space=pltpu.SMEM)
F32 = jnp.float32
BF16 = jnp.bfloat16


def dot(a, b):
    return jnp.dot(a, b, preferred_element_type=F32)


def dot_t(a, b):
    return lax.dot_general(a, b, (((1,), (1,)), ((), ())), preferred_element_type=F32)


def spot_of(device, count):
    z, y = device // 4, (device // 2) % 2
    return z + y * (count // 2 - 1 - 2 * z)


def device_at(spot, core, count):
    y = spot // (count // 4)
    return (spot + y * (count // 2 - 1 - 2 * spot)) * 4 + y * 2 + core


def ring_pairs(count):
    ring = count // 2
    pairs = []
    for spot in range(ring):
        pairs.append((device_at(spot, 0, count), device_at((spot + 1) % ring, 0, count)))
        pairs.append((device_at(spot, 1, count), device_at((spot - 1) % ring, 1, count)))
    return pairs


def ring_tags(count):
    tags = [(0, 0, 0), (0, 0, 1)]
    for step in range(1, count // 4 + 1):
        tags += [(step, 0, 0), (step, 1, 1)]
        if step < count // 4:
            tags += [(step, 0, 1), (step, 1, 0)]
    return tags


def after(shard, gate, found):
    if gate is None:
        return shard
    return lax.optimization_barrier((shard, gate(found)))[0]


def gather_ring(own, count, gates):
    ring = ring_pairs(count)
    cores = [(i, i ^ 1) for i in range(count)]
    last = count // 4
    found = [own, lax.ppermute(own, "tm", cores)]
    streams = list(found)
    for step in range(1, last + 1):
        for stream in range(2 if step < last else 1):
            shard = lax.ppermute(after(streams[stream], gates.get((stream, step, 0)), found), "tm", ring)
            streams[stream] = shard
            found.append(shard)
            found.append(lax.ppermute(after(shard, gates.get((stream, step, 1)), found), "tm", cores))
    return found


def shard_owner(tag, device, count):
    step, swapped, flip = tag
    core = device % 2
    ring = count // 2
    away = (1 - 2 * core) * ((1 - 2 * swapped) * step)
    spot = (spot_of(device, count) - away + ring) % ring
    return device_at(spot, (core + flip) % 2, count)


def prepare_kernel(start, *refs):
    *parts, gain_ref, wide_ref, lat_ref = refs
    _, rows, width, chans = parts[0].shape
    frames = wide_ref.shape[0]
    groups = len(parts)
    mine = lax.axis_index("rows")
    gain = gain_ref[...]
    column = lax.broadcasted_iota(jnp.int32, (rows * width, 1), 0) % width
    edge = jnp.zeros((width, 3 * chans), BF16)
    for frame in range(frames):
        wide_ref[frame, 0] = edge
        wide_ref[frame, groups * rows + 1] = edge
    for at, part in enumerate(parts):
        first = at * rows
        if groups == 2:
            first = (mine if at == 0 else 1 - mine) * rows
        for frame in range(frames):
            raw = part[start + frame]
            lat_ref[frame, pl.ds(first, rows)] = raw
            x = raw.reshape(rows * width, chans).astype(F32)
            y = x * lax.rsqrt(jnp.mean(x * x, axis=-1, keepdims=True) + 1e-06) * gain
            before = jnp.where(column == 0, 0.0, pltpu.roll(y, 1, 0))
            after = jnp.where(column == width - 1, 0.0, pltpu.roll(y, rows * width - 1, 0))
            for dx, v in enumerate((before, y, after)):
                wide_ref[frame, pl.ds(first + 1, rows), :, dx * chans : (dx + 1) * chans] = v.astype(
                    BF16
                ).reshape(rows, width, chans)


def order_kernel(tags, time_ref, head_ref, tail_ref):
    block = time_ref.shape[1] // len(tags)
    device = lax.axis_index("tm")
    for slot, tag in enumerate(tags):
        owner = tag
        if isinstance(tag, tuple):
            owner = shard_owner(tag, device, len(tags))
        source = pl.ds(pl.multiple_of(owner * block, block), block)
        to_ref, at = head_ref, slot * block
        if at >= head_ref.shape[1]:
            to_ref, at = tail_ref, at - head_ref.shape[1]
        for back in range(3):
            to_ref[back, at : at + block] = time_ref[back, source]


def convolve(wide_ref, shards):
    frames, height, width, wide = wide_ref.shape
    height -= 2
    total = None
    for dy in range(3):
        weights = jnp.concatenate(
            [jnp.concatenate([shard[dy, dx] for dx in range(3)], axis=-1) for shard in shards], axis=0
        )
        lhs = wide_ref[:, dy : dy + height].reshape(frames * height * width, wide)
        part = dot_t(lhs, weights)
        total = part if total is None else total + part
    acts = (total * jax.nn.sigmoid(total)).astype(BF16)
    return acts.reshape(frames, height * width, -1)


def keep(flag, values):
    return jnp.where(flag, values, jnp.zeros_like(values))


def temporal(acts, clips, weights, frames):
    first = lax.axis_index("tm") * frames
    spots, width = acts[0].shape
    lines = []
    for t in range(frames):
        line = [acts[t]]
        for back in (1, 2):
            if t < back:
                line.append(jnp.zeros((spots, width), BF16))
            else:
                line.append(keep(clips[first + t - back] == clips[first + t], acts[t - back]))
        lines.append(jnp.concatenate(line, axis=-1))
    lhs = jnp.concatenate(lines, axis=0)
    rhs = jnp.concatenate([weights[k] for k in range(3)], axis=0)
    return dot(lhs, rhs)


def packet_sums(acts, clips, weights, frames, lat=None):
    first = lax.axis_index("tm") * frames
    end = clips.shape[0] - 1
    next0 = clips[jnp.minimum(first + frames, end)]
    next1 = clips[jnp.minimum(first + frames + 1, end)]
    spots, width = acts[0].shape
    sums = [jnp.zeros((spots, width), F32) for _ in range(3)]
    base = None if lat is None else jnp.zeros(lat[0].shape, F32)
    for t in range(frames):
        inside = clips[first + t] == next0
        if lat is not None:
            base = base + keep(inside, lat[t].astype(F32))
        for back in range(min(3, t + 1)):
            both = jnp.logical_and(inside, clips[first + t - back] == next0)
            sums[back] = sums[back] + keep(both, acts[t - back].astype(F32))
    sums = [s.astype(BF16) for s in sums]
    last0 = keep(clips[first + frames - 1] == next0, acts[frames - 1])
    prev0 = keep(clips[first + frames - 2] == next0, acts[frames - 2])
    last1 = keep(clips[first + frames - 1] == next1, acts[frames - 1])
    by0 = dot(sums[0], weights[0])
    by1 = dot(jnp.concatenate([last0, sums[1]], axis=0), weights[1])
    by2 = dot(jnp.concatenate([prev0, last1, sums[2]], axis=0), weights[2])
    total = by0 + by1[spots:] + by2[2 * spots :]
    if base is not None:
        total = total + base
    return by1[:spots] + by2[:spots], by2[spots : 2 * spots], total


def early_kernel(wide_ref, *refs):
    *shards, acts_ref = refs
    acts_ref[...] = convolve(wide_ref, shards)


def first_kernel(lat0_ref, lat1_ref, acts0_ref, acts1_ref, clips, weights, rest_ref, packet_ref):
    acts = [ref[t] for ref in (acts0_ref, acts1_ref) for t in range(ref.shape[0])]
    lat = [ref[t].reshape(acts[0].shape[0], -1) for ref in (lat0_ref, lat1_ref) for t in range(ref.shape[0])]
    frames = len(acts)
    for i, part in enumerate(packet_sums(acts, clips, weights, frames, lat)):
        packet_ref[i] = part
    rest = temporal(acts, clips, weights, frames).reshape(rest_ref.shape)
    for t in range(frames):
        rest_ref[t] = rest[t] + lat[t].astype(F32)


def late_kernel(wide0_ref, wide1_ref, clips, weights, early_ref, *refs):
    *shards, acts_ref, packet_ref = refs
    half, frames = wide0_ref.shape[0], acts_ref.shape[0]
    acts_ref[:half] = convolve(wide0_ref, shards)
    acts_ref[half:] = convolve(wide1_ref, shards)
    acts = [acts_ref[t] for t in range(frames)]
    for i, part in enumerate(packet_sums(acts, clips, weights, frames)):
        packet_ref[i] = (early_ref[i] + part).astype(BF16)


def rest_kernel(acts_ref, clips, weights, early_ref, rest_ref):
    frames = acts_ref.shape[0]
    part = temporal([acts_ref[t] for t in range(frames)], clips, weights, frames)
    rest_ref[...] = early_ref[...] + part.reshape(rest_ref.shape)


def attend_kernel(rest_ref, packet_ref, clips, gain_ref, qkv_ref, proj_ref, out_ref, mixed_ref, normed_ref):
    frames, rows, width, chans = out_ref.shape
    height = mixed_ref.shape[1]
    spots = height * width
    own = rows * width
    first = lax.axis_index("tm") * frames
    mine = pl.ds(lax.axis_index("rows") * rows, rows)
    gain = gain_ref[...]

    number = jnp.int32(1)
    for back in range(1, LONGEST):
        at = first - back
        hit = jnp.logical_and(at >= 0, clips[jnp.maximum(at, 0)] == clips[first])
        number = number + hit.astype(jnp.int32)
    running = packet_ref[2].astype(F32)
    for t in range(frames):
        resid = rest_ref[t]
        if t < 2:
            resid = resid + packet_ref[t].astype(F32)
        if t > 0:
            same = clips[first + t] == clips[first + t - 1]
            running = keep(same, running)
            number = jnp.where(same, number + 1, 1)
        running = running + resid
        mixed = (resid + running / jnp.full((1, chans), number.astype(F32))).astype(BF16)
        mixed_ref[t] = mixed.reshape(height, width, chans)
        x = mixed.astype(F32)
        y = x * lax.rsqrt(jnp.mean(x * x, axis=-1, keepdims=True) + 1e-06) * gain
        normed_ref[t] = y.astype(BF16).reshape(height, width, chans)

    query = dot(normed_ref[:, mine].reshape(frames * own, chans), qkv_ref[:, :chans]).astype(BF16)
    both = dot(normed_ref[...].reshape(frames * spots, chans), qkv_ref[:, chans:]).astype(BF16)
    attended = []
    for t in range(frames):
        key = both[t * spots : (t + 1) * spots, :chans]
        value = both[t * spots : (t + 1) * spots, chans:]
        scores = dot_t(query[t * own : (t + 1) * own], key) * chans ** (-0.5)
        weights = jnp.exp(scores - jnp.max(scores, axis=-1, keepdims=True))
        probs = (weights / jnp.sum(weights, axis=-1, keepdims=True)).astype(BF16)
        attended.append(dot(probs, value).astype(BF16))
    result = dot(jnp.concatenate(attended, axis=0), proj_ref[...])
    result = result + mixed_ref[:, mine].reshape(frames * own, chans).astype(F32)
    out_ref[...] = result.astype(BF16).reshape(frames, rows, width, chans)


def local(latents, clip_ids, gain_in, w_space, w_time, gain_attn, w_qkv, w_out):
    frames, rows, width, chans = latents.shape
    groups, count = lax.axis_size("rows"), lax.axis_size("tm")
    height = groups * rows
    spots = height * width
    shape = jax.ShapeDtypeStruct
    params = pltpu.CompilerParams(vmem_limit_bytes=(28 if frames * spots <= 1024 else 60) << 20)
    assert frames + 1 >= LONGEST

    half = frames // 2
    if groups == 2:
        parts = [latents, lax.ppermute(latents, "rows", [(0, 1), (1, 0)])]
    else:
        everything = lax.all_gather(latents, "rows")
        parts = [everything[i] for i in range(groups)]

    shard = jnp.transpose(w_space, (0, 1, 3, 2))
    ringed = shard.shape[2] % 16 == 0 and count % 8 == 0
    tags = ring_tags(count) if ringed else [0, 1]
    cut = len(tags) // 2
    split = cut * (chans // len(tags))

    gain = gain_in.reshape(1, chans)
    prepared = [
        pl.pallas_call(
            functools.partial(prepare_kernel, start),
            out_shape=(
                shape((half, height + 2, width, 3 * chans), BF16),
                shape((half, height, width, chans), BF16),
            ),
            in_specs=[VMEM] * (groups + 1),
            out_specs=(VMEM, VMEM),
            compiler_params=params,
            name="prepare",
        )(*parts, gain)
        for start in (0, half)
    ]
    wides = [pair[0] for pair in prepared]
    lats = [pair[1] for pair in prepared]
    head, tail = pl.pallas_call(
        functools.partial(order_kernel, tags),
        out_shape=(shape((3, split, chans), BF16), shape((3, chans - split, chans), BF16)),
        in_specs=[VMEM],
        out_specs=(VMEM, VMEM),
        compiler_params=params,
        name="order",
    )(w_time)

    acts = [None, None]
    first = []

    def early(which, shards):
        acts[which] = pl.pallas_call(
            early_kernel,
            out_shape=shape((half, spots, split), BF16),
            in_specs=[VMEM] * (1 + cut),
            out_specs=VMEM,
            compiler_params=params,
            name="early",
        )(wides[which], *shards[:cut])
        return acts[which]

    def begin(found):
        for which in range(2):
            if acts[which] is None:
                early(which, found)
        first.extend(
            pl.pallas_call(
                first_kernel,
                out_shape=(shape((frames, spots, chans), F32), shape((3, spots, chans), F32)),
                in_specs=[VMEM] * 4 + [SMEM, VMEM],
                out_specs=(VMEM, VMEM),
                compiler_params=params,
                name="first",
            )(*lats, *acts, clip_ids, head)
        )
        return first[1]

    if ringed:
        last = count // 4
        gates = {
            (0, 2, 0): lambda found: tail,
            (0, last - 1, 0): lambda found: parts[1],
            (1, last - 1, 0): functools.partial(early, 0),
            (0, last, 0): functools.partial(early, 1),
        }
        shards = gather_ring(shard, count, gates)
    else:
        whole = lax.all_gather(shard, "tm", axis=2, tiled=True)
        shards = [whole[:, :, :split], whole[:, :, split:]]
    if not first:
        begin(shards)
    rest, packet = first
    acts, packet = pl.pallas_call(
        late_kernel,
        out_shape=(shape((frames, spots, chans - split), BF16), shape((3, spots, chans), BF16)),
        in_specs=[VMEM, VMEM, SMEM, VMEM, VMEM] + [VMEM] * (len(tags) - cut),
        out_specs=(VMEM, VMEM),
        compiler_params=params,
        name="late",
    )(*wides, clip_ids, tail, packet, *shards[cut:])
    packet = lax.ppermute(packet, "tm", [(i, i + 1) for i in range(count - 1)])
    rest = pl.pallas_call(
        rest_kernel,
        out_shape=shape((frames, spots, chans), F32),
        in_specs=[VMEM, SMEM, VMEM, VMEM],
        out_specs=VMEM,
        compiler_params=params,
        name="rest",
    )(acts, clip_ids, tail, rest)
    return pl.pallas_call(
        attend_kernel,
        out_shape=shape((frames, rows, width, chans), BF16),
        in_specs=[VMEM, VMEM, SMEM, VMEM, VMEM, VMEM],
        out_specs=VMEM,
        scratch_shapes=[
            pltpu.VMEM((frames, height, width, chans), BF16),
            pltpu.VMEM((frames, height, width, chans), BF16),
        ],
        compiler_params=params,
        name="attend",
    )(rest, packet, clip_ids, gain_attn.reshape(1, chans), w_qkv, w_out)


def solution(mesh):
    placed = (P("tm", "rows", None, None), P(), P(), P(None, None, None, "tm"), P(), P(), P(), P())
    return jax.shard_map(
        local, mesh=mesh, in_specs=placed, out_specs=P("tm", "rows", None, None), check_vma=False
    )
```

```python
import functools

import jax
import jax.numpy as jnp
from jax import lax
from jax.experimental import pallas as pl
from jax.experimental.pallas import tpu as pltpu
from jax.sharding import PartitionSpec as P

LONGEST = 9
VMEM = pl.BlockSpec(memory_space=pltpu.VMEM)
SMEM = pl.BlockSpec(memory_space=pltpu.SMEM)
F32 = jnp.float32
BF16 = jnp.bfloat16


def dot(a, b):
    return jnp.dot(a, b, preferred_element_type=F32)


def dot_t(a, b):
    return lax.dot_general(a, b, (((1,), (1,)), ((), ())), preferred_element_type=F32)


def spot_of(device, count):
    z, y = device // 4, (device // 2) % 2
    return z + y * (count // 2 - 1 - 2 * z)


def device_at(spot, core, count):
    y = spot // (count // 4)
    return (spot + y * (count // 2 - 1 - 2 * spot)) * 4 + y * 2 + core


def ring_pairs(count):
    ring = count // 2
    pairs = []
    for spot in range(ring):
        pairs.append((device_at(spot, 0, count), device_at((spot + 1) % ring, 0, count)))
        pairs.append((device_at(spot, 1, count), device_at((spot - 1) % ring, 1, count)))
    return pairs


def ring_tags(count):
    tags = [(0, 0, 0), (0, 0, 1)]
    for step in range(1, count // 4 + 1):
        tags += [(step, 0, 0), (step, 1, 1)]
        if step < count // 4:
            tags += [(step, 0, 1), (step, 1, 0)]
    return tags


def after(shard, gate, found):
    if gate is None:
        return shard
    return lax.optimization_barrier((shard, gate(found)))[0]


def gather_ring(own, count, gates):
    ring = ring_pairs(count)
    cores = [(i, i ^ 1) for i in range(count)]
    last = count // 4
    found = [own, lax.ppermute(own, "tm", cores)]
    streams = list(found)
    for step in range(1, last + 1):
        for stream in range(2 if step < last else 1):
            shard = lax.ppermute(after(streams[stream], gates.get((stream, step, 0)), found), "tm", ring)
            streams[stream] = shard
            found.append(shard)
            found.append(lax.ppermute(after(shard, gates.get((stream, step, 1)), found), "tm", cores))
    return found


def shard_owner(tag, device, count):
    step, swapped, flip = tag
    core = device % 2
    ring = count // 2
    away = (1 - 2 * core) * ((1 - 2 * swapped) * step)
    spot = (spot_of(device, count) - away + ring) % ring
    return device_at(spot, (core + flip) % 2, count)


def prepare_kernel(start, at, groups, *refs):
    part, gain_ref, wide_ref, lat_ref = *refs[:2], *refs[-2:]
    _, rows, width, chans = part.shape
    frames = wide_ref.shape[0]
    gain = gain_ref[...]
    column = lax.broadcasted_iota(jnp.int32, (rows * width, 1), 0) % width
    edge = jnp.zeros((width, 3 * chans), BF16)
    first = at * rows
    if groups == 2:
        mine = lax.axis_index("rows")
        first = (mine if at == 0 else 1 - mine) * rows
    for frame in range(frames):
        if at == 0:
            wide_ref[frame, 0] = edge
            wide_ref[frame, groups * rows + 1] = edge
        raw = part[start + frame]
        lat_ref[frame, pl.ds(first, rows)] = raw
        x = raw.reshape(rows * width, chans).astype(F32)
        y = x * lax.rsqrt(jnp.mean(x * x, axis=-1, keepdims=True) + 1e-06) * gain
        before = jnp.where(column == 0, 0.0, pltpu.roll(y, 1, 0))
        after = jnp.where(column == width - 1, 0.0, pltpu.roll(y, rows * width - 1, 0))
        for dx, v in enumerate((before, y, after)):
            wide_ref[frame, pl.ds(first + 1, rows), :, dx * chans : (dx + 1) * chans] = v.astype(
                BF16
            ).reshape(rows, width, chans)


def ordered(time_ref, tags, slots):
    block = time_ref.shape[1] // slots
    device = lax.axis_index("tm")
    rows = []
    for tag in tags:
        owner = shard_owner(tag, device, slots) if isinstance(tag, tuple) else tag
        rows.append(pl.ds(pl.multiple_of(owner * block, block), block))
    return [jnp.concatenate([time_ref[back, row] for row in rows], axis=0) for back in range(3)]


def convolve(wide_ref, shards):
    frames, height, width, wide = wide_ref.shape
    height -= 2
    total = None
    for dy in range(3):
        weights = jnp.concatenate(
            [jnp.concatenate([shard[dy, dx] for dx in range(3)], axis=-1) for shard in shards], axis=0
        )
        lhs = wide_ref[:, dy : dy + height].reshape(frames * height * width, wide)
        part = dot_t(lhs, weights)
        total = part if total is None else total + part
    acts = (total * jax.nn.sigmoid(total)).astype(BF16)
    return acts.reshape(frames, height * width, -1)


def keep(flag, values):
    return jnp.where(flag, values, jnp.zeros_like(values))


def temporal(acts, clips, weights, frames):
    first = lax.axis_index("tm") * frames
    spots, width = acts[0].shape
    lines = []
    for t in range(frames):
        line = [acts[t]]
        for back in (1, 2):
            if t < back:
                line.append(jnp.zeros((spots, width), BF16))
            else:
                line.append(keep(clips[first + t - back] == clips[first + t], acts[t - back]))
        lines.append(jnp.concatenate(line, axis=-1))
    lhs = jnp.concatenate(lines, axis=0)
    rhs = jnp.concatenate([weights[k] for k in range(3)], axis=0)
    return dot(lhs, rhs)


def packet_sums(acts, clips, weights, frames, lat=None):
    first = lax.axis_index("tm") * frames
    end = clips.shape[0] - 1
    next0 = clips[jnp.minimum(first + frames, end)]
    next1 = clips[jnp.minimum(first + frames + 1, end)]
    spots, width = acts[0].shape
    sums = [jnp.zeros((spots, width), F32) for _ in range(3)]
    base = None if lat is None else jnp.zeros(lat[0].shape, F32)
    for t in range(frames):
        inside = clips[first + t] == next0
        if lat is not None:
            base = base + keep(inside, lat[t].astype(F32))
        for back in range(min(3, t + 1)):
            both = jnp.logical_and(inside, clips[first + t - back] == next0)
            sums[back] = sums[back] + keep(both, acts[t - back].astype(F32))
    sums = [s.astype(BF16) for s in sums]
    last0 = keep(clips[first + frames - 1] == next0, acts[frames - 1])
    prev0 = keep(clips[first + frames - 2] == next0, acts[frames - 2])
    last1 = keep(clips[first + frames - 1] == next1, acts[frames - 1])
    by0 = dot(sums[0], weights[0])
    by1 = dot(jnp.concatenate([last0, sums[1]], axis=0), weights[1])
    by2 = dot(jnp.concatenate([prev0, last1, sums[2]], axis=0), weights[2])
    total = by0 + by1[spots:] + by2[2 * spots :]
    if base is not None:
        total = total + base
    return by1[:spots] + by2[:spots], by2[spots : 2 * spots], total


def early_kernel(wide_ref, *refs):
    *shards, acts_ref = refs
    acts_ref[...] = convolve(wide_ref, shards)


def first_kernel(tags, slots, lat0_ref, lat1_ref, acts0_ref, acts1_ref, clips, time_ref, rest_ref, packet_ref):
    weights = ordered(time_ref, tags, slots)
    acts = [ref[t] for ref in (acts0_ref, acts1_ref) for t in range(ref.shape[0])]
    lat = [ref[t].reshape(acts[0].shape[0], -1) for ref in (lat0_ref, lat1_ref) for t in range(ref.shape[0])]
    frames = len(acts)
    for i, part in enumerate(packet_sums(acts, clips, weights, frames, lat)):
        packet_ref[i] = part
    rest = temporal(acts, clips, weights, frames).reshape(rest_ref.shape)
    for t in range(frames):
        rest_ref[t] = rest[t] + lat[t].astype(F32)


def late_kernel(tags, slots, wide0_ref, wide1_ref, clips, time_ref, early_ref, *refs):
    *shards, acts_ref, packet_ref = refs
    half, frames = wide0_ref.shape[0], acts_ref.shape[0]
    acts_ref[:half] = convolve(wide0_ref, shards)
    acts_ref[half:] = convolve(wide1_ref, shards)
    acts = [acts_ref[t] for t in range(frames)]
    weights = ordered(time_ref, tags, slots)
    for i, part in enumerate(packet_sums(acts, clips, weights, frames)):
        packet_ref[i] = (early_ref[i] + part).astype(BF16)


def places(clips, frames):
    first = lax.axis_index("tm") * frames
    number = jnp.int32(1)
    for back in range(1, LONGEST):
        at = first - back
        hit = jnp.logical_and(at >= 0, clips[jnp.maximum(at, 0)] == clips[first])
        number = number + hit.astype(jnp.int32)
    found = [(None, clips[first] == clips[first], number)]
    for t in range(1, frames):
        same = clips[first + t] == clips[first + t - 1]
        number = jnp.where(same, number + 1, 1)
        found.append((same, clips[first + t] == clips[first], number))
    return found


def share(number, chans):
    return 1.0 / jnp.full((1, chans), number.astype(F32))


def rest_kernel(tags, slots, acts_ref, clips, time_ref, early_ref, base_ref):
    frames, spots, chans = base_ref.shape
    weights = ordered(time_ref, tags, slots)
    part = temporal([acts_ref[t] for t in range(frames)], clips, weights, frames)
    running = None
    for t, (same, _, number) in enumerate(places(clips, frames)):
        resid = early_ref[t] + part[t * spots : (t + 1) * spots]
        running = resid if t == 0 else keep(same, running) + resid
        base_ref[t] = resid + running * share(number, chans)


def attend_kernel(base_ref, packet_ref, clips, gain_ref, qkv_ref, proj_ref, out_ref, mixed_ref, normed_ref):
    frames, rows, width, chans = out_ref.shape
    height = mixed_ref.shape[1]
    spots = height * width
    own = rows * width
    mine = pl.ds(lax.axis_index("rows") * rows, rows)
    gain = gain_ref[...]
    place = places(clips, frames)
    step = frames // 2
    joint = 2 if spots <= 128 and step % 2 == 0 else 1
    blocked = (
        lax.broadcasted_iota(jnp.int32, (joint * own, joint * spots), 0) // own
        != lax.broadcasted_iota(jnp.int32, (joint * own, joint * spots), 1) // spots
    )

    terms = [packet_ref[0].astype(F32), packet_ref[1].astype(F32)]
    carried = packet_ref[2].astype(F32) + terms[0]
    for start in range(0, frames, step):
        for t in range(start, start + step):
            if t == 1:
                carried = carried + terms[1]
            _, among, number = place[t]
            mixed = base_ref[t] + carried * keep(among, share(number, chans))
            if t < 2:
                mixed = mixed + terms[t]
            mixed = mixed.astype(BF16)
            mixed_ref[t] = mixed.reshape(height, width, chans)
            x = mixed.astype(F32)
            y = x * lax.rsqrt(jnp.mean(x * x, axis=-1, keepdims=True) + 1e-06) * gain
            normed_ref[t] = y.astype(BF16).reshape(height, width, chans)
        span = slice(start, start + step)
        query = dot(normed_ref[span, mine].reshape(step * own, chans), qkv_ref[:, :chans]).astype(BF16)
        both = dot(normed_ref[span].reshape(step * spots, chans), qkv_ref[:, chans:]).astype(BF16)
        attended = []
        for t in range(0, step, joint):
            key = both[t * spots : (t + joint) * spots, :chans]
            value = both[t * spots : (t + joint) * spots, chans:]
            scores = dot_t(query[t * own : (t + joint) * own], key) * chans ** (-0.5)
            if joint > 1:
                scores = jnp.where(blocked, -jnp.inf, scores)
            weights = jnp.exp(scores - jnp.max(scores, axis=-1, keepdims=True))
            probs = (weights / jnp.sum(weights, axis=-1, keepdims=True)).astype(BF16)
            attended.append(dot(probs, value).astype(BF16))
        result = dot(jnp.concatenate(attended, axis=0), proj_ref[...])
        result = result + mixed_ref[span, mine].reshape(step * own, chans).astype(F32)
        out_ref[span] = result.astype(BF16).reshape(step, rows, width, chans)


def local(latents, clip_ids, gain_in, w_space, w_time, gain_attn, w_qkv, w_out):
    frames, rows, width, chans = latents.shape
    groups, count = lax.axis_size("rows"), lax.axis_size("tm")
    height = groups * rows
    spots = height * width
    shape = jax.ShapeDtypeStruct
    params = pltpu.CompilerParams(vmem_limit_bytes=(28 if frames * spots <= 1024 else 60) << 20)
    assert frames + 1 >= LONGEST

    half = frames // 2
    if groups == 2:
        parts = [latents, lax.ppermute(latents, "rows", [(0, 1), (1, 0)])]
    else:
        everything = lax.all_gather(latents, "rows")
        parts = [everything[i] for i in range(groups)]

    shard = jnp.transpose(w_space, (0, 1, 3, 2))
    ringed = shard.shape[2] % 16 == 0 and count % 8 == 0
    tags = ring_tags(count) if ringed else [0, 1]
    cut = len(tags) // 2
    split = cut * (chans // len(tags))

    gain = gain_in.reshape(1, chans)
    prepared = []
    own = []
    for start in (0, half):
        pair = ()
        for at, part in enumerate(parts):
            pair = pl.pallas_call(
                functools.partial(prepare_kernel, start, at, groups),
                out_shape=(
                    shape((half, height + 2, width, 3 * chans), BF16),
                    shape((half, height, width, chans), BF16),
                ),
                in_specs=[VMEM] * (2 + len(pair)),
                out_specs=(VMEM, VMEM),
                input_output_aliases={2: 0, 3: 1} if pair else {},
                compiler_params=params,
                name="prepare",
            )(part, gain, *pair)
            if at == 0:
                own.append(pair)
        prepared.append(pair)
    wides = [pair[0] for pair in prepared]
    lats = [pair[1] for pair in prepared]
    acts = [None, None]
    first = []

    def early(which, shards):
        acts[which] = pl.pallas_call(
            early_kernel,
            out_shape=shape((half, spots, split), BF16),
            in_specs=[VMEM] * (1 + cut),
            out_specs=VMEM,
            compiler_params=params,
            name="early",
        )(wides[which], *shards[:cut])
        return acts[which]

    def begin(found):
        for which in range(2):
            if acts[which] is None:
                early(which, found)
        first.extend(
            pl.pallas_call(
                functools.partial(first_kernel, tags[:cut], len(tags)),
                out_shape=(shape((frames, spots, chans), F32), shape((3, spots, chans), F32)),
                in_specs=[VMEM] * 4 + [SMEM, VMEM],
                out_specs=(VMEM, VMEM),
                compiler_params=params,
                name="first",
            )(*lats, *acts, clip_ids, w_time)
        )
        return first[1]

    if ringed:
        last = count // 4
        gates = {
            (1, 1, 1): lambda found: own,
            (1, last - 2, 1): lambda found: parts[1],
            (1, last - 1, 0): functools.partial(early, 0),
            (1, last - 1, 1): lambda found: found[9],
            (0, last, 0): functools.partial(early, 1),
            (0, last, 1): begin,
        }
        shards = gather_ring(shard, count, gates)
    else:
        whole = lax.all_gather(shard, "tm", axis=2, tiled=True)
        shards = [whole[:, :, :split], whole[:, :, split:]]
    if not first:
        begin(shards)
    rest, packet = first
    acts, packet = pl.pallas_call(
        functools.partial(late_kernel, tags[cut:], len(tags)),
        out_shape=(shape((frames, spots, chans - split), BF16), shape((3, spots, chans), BF16)),
        in_specs=[VMEM, VMEM, SMEM, VMEM, VMEM] + [VMEM] * (len(tags) - cut),
        out_specs=(VMEM, VMEM),
        compiler_params=params,
        name="late",
    )(*wides, clip_ids, w_time, packet, *shards[cut:])
    packet = lax.ppermute(packet, "tm", [(i, i + 1) for i in range(count - 1)])
    rest = pl.pallas_call(
        functools.partial(rest_kernel, tags[cut:], len(tags)),
        out_shape=shape((frames, spots, chans), F32),
        in_specs=[VMEM, SMEM, VMEM, VMEM],
        out_specs=VMEM,
        compiler_params=params,
        name="rest",
    )(acts, clip_ids, w_time, rest)
    return pl.pallas_call(
        attend_kernel,
        out_shape=shape((frames, rows, width, chans), BF16),
        in_specs=[VMEM, VMEM, SMEM, VMEM, VMEM, VMEM],
        out_specs=VMEM,
        scratch_shapes=[
            pltpu.VMEM((frames, height, width, chans), BF16),
            pltpu.VMEM((frames, height, width, chans), BF16),
        ],
        compiler_params=params,
        name="attend",
    )(rest, packet, clip_ids, gain_attn.reshape(1, chans), w_qkv, w_out)


def solution(mesh):
    placed = (P("tm", "rows", None, None), P(), P(), P(None, None, None, "tm"), P(), P(), P(), P())
    return jax.shard_map(
        local, mesh=mesh, in_specs=placed, out_specs=P("tm", "rows", None, None), check_vma=False
    )
```

```python
import functools

import jax
import jax.numpy as jnp
from jax import lax
from jax.experimental import pallas as pl
from jax.experimental.pallas import tpu as pltpu
from jax.sharding import PartitionSpec as P

LONGEST = 9
VMEM = pl.BlockSpec(memory_space=pltpu.VMEM)
SMEM = pl.BlockSpec(memory_space=pltpu.SMEM)
F32 = jnp.float32
BF16 = jnp.bfloat16


def dot(a, b):
    return jnp.dot(a, b, preferred_element_type=F32)


def dot_t(a, b):
    return lax.dot_general(a, b, (((1,), (1,)), ((), ())), preferred_element_type=F32)


def spot_of(device, count):
    z, y = device // 4, (device // 2) % 2
    return z + y * (count // 2 - 1 - 2 * z)


def device_at(spot, core, count):
    y = spot // (count // 4)
    return (spot + y * (count // 2 - 1 - 2 * spot)) * 4 + y * 2 + core


def ring_pairs(count):
    ring = count // 2
    pairs = []
    for spot in range(ring):
        pairs.append((device_at(spot, 0, count), device_at((spot + 1) % ring, 0, count)))
        pairs.append((device_at(spot, 1, count), device_at((spot - 1) % ring, 1, count)))
    return pairs


def ring_tags(count):
    tags = [(0, 0, 0), (0, 0, 1)]
    for step in range(1, count // 4 + 1):
        tags += [(step, 0, 0), (step, 1, 1)]
        if step < count // 4:
            tags += [(step, 0, 1), (step, 1, 0)]
    return tags


def after(shard, gate, found):
    if gate is None:
        return shard
    return lax.optimization_barrier((shard, gate(found)))[0]


def gather_ring(own, count, gates):
    ring = ring_pairs(count)
    cores = [(i, i ^ 1) for i in range(count)]
    last = count // 4
    found = [own, lax.ppermute(own, "tm", cores)]
    streams = list(found)
    for step in range(1, last + 1):
        for stream in range(2 if step < last else 1):
            shard = lax.ppermute(after(streams[stream], gates.get((stream, step, 0)), found), "tm", ring)
            streams[stream] = shard
            found.append(shard)
            found.append(lax.ppermute(after(shard, gates.get((stream, step, 1)), found), "tm", cores))
    return found


def shard_owner(tag, device, count):
    step, swapped, flip = tag
    core = device % 2
    ring = count // 2
    away = (1 - 2 * core) * ((1 - 2 * swapped) * step)
    spot = (spot_of(device, count) - away + ring) % ring
    return device_at(spot, (core + flip) % 2, count)


def prepare_kernel(start, at, groups, *refs):
    part, gain_ref, wide_ref, lat_ref = *refs[:2], *refs[-2:]
    _, rows, width, chans = part.shape
    frames = wide_ref.shape[0]
    gain = gain_ref[...]
    column = lax.broadcasted_iota(jnp.int32, (rows * width, 1), 0) % width
    edge = jnp.zeros((width, 3 * chans), BF16)
    first = at * rows
    if groups == 2:
        mine = lax.axis_index("rows")
        first = (mine if at == 0 else 1 - mine) * rows
    for frame in range(frames):
        if at == 0:
            wide_ref[frame, 0] = edge
            wide_ref[frame, groups * rows + 1] = edge
        raw = part[start + frame]
        lat_ref[frame, pl.ds(first, rows)] = raw
        x = raw.reshape(rows * width, chans).astype(F32)
        y = x * lax.rsqrt(jnp.mean(x * x, axis=-1, keepdims=True) + 1e-06) * gain
        before = jnp.where(column == 0, 0.0, pltpu.roll(y, 1, 0))
        after = jnp.where(column == width - 1, 0.0, pltpu.roll(y, rows * width - 1, 0))
        for dx, v in enumerate((before, y, after)):
            wide_ref[frame, pl.ds(first + 1, rows), :, dx * chans : (dx + 1) * chans] = v.astype(
                BF16
            ).reshape(rows, width, chans)


def ordered(time_ref, tags, slots):
    block = time_ref.shape[1] // slots
    device = lax.axis_index("tm")
    rows = []
    for tag in tags:
        owner = shard_owner(tag, device, slots) if isinstance(tag, tuple) else tag
        rows.append(pl.ds(pl.multiple_of(owner * block, block), block))
    return [jnp.concatenate([time_ref[back, row] for row in rows], axis=0) for back in range(3)]


def convolve(wide_ref, shards):
    frames, height, width, wide = wide_ref.shape
    height -= 2
    total = None
    for dy in range(3):
        weights = jnp.concatenate(
            [jnp.concatenate([shard[dy, dx] for dx in range(3)], axis=-1) for shard in shards], axis=0
        )
        lhs = wide_ref[:, dy : dy + height].reshape(frames * height * width, wide)
        part = dot_t(lhs, weights)
        total = part if total is None else total + part
    acts = (total * jax.nn.sigmoid(total)).astype(BF16)
    return acts.reshape(frames, height * width, -1)


def keep(flag, values):
    return jnp.where(flag, values, jnp.zeros_like(values))


def temporal(acts, clips, weights, frames):
    first = lax.axis_index("tm") * frames
    spots, width = acts[0].shape
    lines = []
    for t in range(frames):
        line = [acts[t]]
        for back in (1, 2):
            if t < back:
                line.append(jnp.zeros((spots, width), BF16))
            else:
                line.append(keep(clips[first + t - back] == clips[first + t], acts[t - back]))
        lines.append(jnp.concatenate(line, axis=-1))
    lhs = jnp.concatenate(lines, axis=0)
    rhs = jnp.concatenate([weights[k] for k in range(3)], axis=0)
    return dot(lhs, rhs)


def packet_sums(acts, clips, weights, frames, lat=None):
    first = lax.axis_index("tm") * frames
    end = clips.shape[0] - 1
    next0 = clips[jnp.minimum(first + frames, end)]
    next1 = clips[jnp.minimum(first + frames + 1, end)]
    spots, width = acts[0].shape
    sums = [jnp.zeros((spots, width), F32) for _ in range(3)]
    base = None if lat is None else jnp.zeros(lat[0].shape, F32)
    for t in range(frames):
        inside = clips[first + t] == next0
        if lat is not None:
            base = base + keep(inside, lat[t].astype(F32))
        for back in range(min(3, t + 1)):
            both = jnp.logical_and(inside, clips[first + t - back] == next0)
            sums[back] = sums[back] + keep(both, acts[t - back].astype(F32))
    sums = [s.astype(BF16) for s in sums]
    last0 = keep(clips[first + frames - 1] == next0, acts[frames - 1])
    prev0 = keep(clips[first + frames - 2] == next0, acts[frames - 2])
    last1 = keep(clips[first + frames - 1] == next1, acts[frames - 1])
    by0 = dot(sums[0], weights[0])
    by1 = dot(jnp.concatenate([last0, sums[1]], axis=0), weights[1])
    by2 = dot(jnp.concatenate([prev0, last1, sums[2]], axis=0), weights[2])
    total = by0 + by1[spots:] + by2[2 * spots :]
    if base is not None:
        total = total + base
    return by1[:spots] + by2[:spots], by2[spots : 2 * spots], total


def early_kernel(wide_ref, *refs):
    *shards, acts_ref = refs
    acts_ref[...] = convolve(wide_ref, shards)


def first_kernel(tags, slots, lat0_ref, lat1_ref, acts0_ref, acts1_ref, clips, time_ref, rest_ref, packet_ref):
    weights = ordered(time_ref, tags, slots)
    acts = [ref[t] for ref in (acts0_ref, acts1_ref) for t in range(ref.shape[0])]
    lat = [ref[t].reshape(acts[0].shape[0], -1) for ref in (lat0_ref, lat1_ref) for t in range(ref.shape[0])]
    frames = len(acts)
    for i, part in enumerate(packet_sums(acts, clips, weights, frames, lat)):
        packet_ref[i] = part
    rest = temporal(acts, clips, weights, frames).reshape(rest_ref.shape)
    for t in range(frames):
        rest_ref[t] = rest[t] + lat[t].astype(F32)


def late_kernel(tags, slots, wide0_ref, wide1_ref, clips, time_ref, early_ref, *refs):
    *shards, acts_ref, packet_ref = refs
    half, frames = wide0_ref.shape[0], acts_ref.shape[0]
    acts_ref[:half] = convolve(wide0_ref, shards)
    acts_ref[half:] = convolve(wide1_ref, shards)
    acts = [acts_ref[t] for t in range(frames)]
    weights = ordered(time_ref, tags, slots)
    for i, part in enumerate(packet_sums(acts, clips, weights, frames)):
        packet_ref[i] = (early_ref[i] + part).astype(BF16)


def places(clips, frames):
    first = lax.axis_index("tm") * frames
    number = jnp.int32(1)
    for back in range(1, LONGEST):
        at = first - back
        hit = jnp.logical_and(at >= 0, clips[jnp.maximum(at, 0)] == clips[first])
        number = number + hit.astype(jnp.int32)
    found = [(None, clips[first] == clips[first], number)]
    for t in range(1, frames):
        same = clips[first + t] == clips[first + t - 1]
        number = jnp.where(same, number + 1, 1)
        found.append((same, clips[first + t] == clips[first], number))
    return found


def share(number, chans):
    return 1.0 / jnp.full((1, chans), number.astype(F32))


def rest_kernel(tags, slots, acts_ref, clips, time_ref, early_ref, base_ref):
    frames, spots, chans = base_ref.shape
    weights = ordered(time_ref, tags, slots)
    part = temporal([acts_ref[t] for t in range(frames)], clips, weights, frames)
    running = None
    for t, (same, _, number) in enumerate(places(clips, frames)):
        resid = early_ref[t] + part[t * spots : (t + 1) * spots]
        running = resid if t == 0 else keep(same, running) + resid
        base_ref[t] = resid + running * share(number, chans)


def attend_kernel(base_ref, packet_ref, clips, gain_ref, qkv_ref, proj_ref, out_ref, mixed_ref, normed_ref):
    frames, rows, width, chans = out_ref.shape
    height = mixed_ref.shape[1]
    spots = height * width
    own = rows * width
    mine = pl.ds(lax.axis_index("rows") * rows, rows)
    gain = gain_ref[...]
    place = places(clips, frames)
    step = frames // 2
    joint = 2 if spots <= 128 and step % 2 == 0 else 1
    blocked = (
        lax.broadcasted_iota(jnp.int32, (joint * own, joint * spots), 0) // own
        != lax.broadcasted_iota(jnp.int32, (joint * own, joint * spots), 1) // spots
    )

    terms = [packet_ref[0].astype(F32), packet_ref[1].astype(F32)]
    carried = packet_ref[2].astype(F32) + terms[0]
    for start in range(0, frames, step):
        for t in range(start, start + step):
            if t == 1:
                carried = carried + terms[1]
            _, among, number = place[t]
            mixed = base_ref[t] + carried * keep(among, share(number, chans))
            if t < 2:
                mixed = mixed + terms[t]
            mixed = mixed.astype(BF16)
            mixed_ref[t] = mixed.reshape(height, width, chans)
            x = mixed.astype(F32)
            y = x * lax.rsqrt(jnp.mean(x * x, axis=-1, keepdims=True) + 1e-06) * gain
            normed_ref[t] = y.astype(BF16).reshape(height, width, chans)
        span = slice(start, start + step)
        query = dot(normed_ref[span, mine].reshape(step * own, chans), qkv_ref[:, :chans]).astype(BF16)
        both = dot(normed_ref[span].reshape(step * spots, chans), qkv_ref[:, chans:]).astype(BF16)
        attended = []
        for t in range(0, step, joint):
            key = both[t * spots : (t + joint) * spots, :chans]
            value = both[t * spots : (t + joint) * spots, chans:]
            scores = dot_t(query[t * own : (t + joint) * own], key) * chans ** (-0.5)
            if joint > 1:
                scores = jnp.where(blocked, -jnp.inf, scores)
            weights = jnp.exp(scores - jnp.max(scores, axis=-1, keepdims=True))
            probs = (weights * (1.0 / jnp.sum(weights, axis=-1, keepdims=True))).astype(BF16)
            attended.append(dot(probs, value).astype(BF16))
        result = dot(jnp.concatenate(attended, axis=0), proj_ref[...])
        result = result + mixed_ref[span, mine].reshape(step * own, chans).astype(F32)
        out_ref[span] = result.astype(BF16).reshape(step, rows, width, chans)


def local(latents, clip_ids, gain_in, w_space, w_time, gain_attn, w_qkv, w_out):
    frames, rows, width, chans = latents.shape
    groups, count = lax.axis_size("rows"), lax.axis_size("tm")
    height = groups * rows
    spots = height * width
    shape = jax.ShapeDtypeStruct
    params = pltpu.CompilerParams(vmem_limit_bytes=(28 if frames * spots <= 1024 else 60) << 20)
    assert frames + 1 >= LONGEST

    half = frames // 2
    if groups == 2:
        parts = [latents, lax.ppermute(latents, "rows", [(0, 1), (1, 0)])]
    else:
        everything = lax.all_gather(latents, "rows")
        parts = [everything[i] for i in range(groups)]

    shard = jnp.transpose(w_space, (0, 1, 3, 2))
    ringed = shard.shape[2] % 16 == 0 and count % 8 == 0
    tags = ring_tags(count) if ringed else [0, 1]
    cut = len(tags) // 2
    split = cut * (chans // len(tags))

    gain = gain_in.reshape(1, chans)
    def prepare(start, at, part, pair=()):
        return pl.pallas_call(
            functools.partial(prepare_kernel, start, at, groups),
            out_shape=(
                shape((half, height + 2, width, 3 * chans), BF16),
                shape((half, height, width, chans), BF16),
            ),
            in_specs=[VMEM] * (2 + len(pair)),
            out_specs=(VMEM, VMEM),
            input_output_aliases={2: 0, 3: 1} if pair else {},
            compiler_params=params,
            name="prepare",
        )(part, gain, *pair)

    own = [prepare(start, 0, parts[0]) for start in (0, half)]
    wides, lats = [None, None], [None, None]

    def prepare_rest(which):
        pair = own[which]
        for at in range(1, groups):
            part = parts[at]
            pair = prepare(which * half, at, part, pair)
        wides[which], lats[which] = pair

    acts = [None, None]
    first = []

    def early(which, shards):
        prepare_rest(which)
        acts[which] = pl.pallas_call(
            early_kernel,
            out_shape=shape((half, spots, split), BF16),
            in_specs=[VMEM] * (1 + cut),
            out_specs=VMEM,
            compiler_params=params,
            name="early",
        )(wides[which], *shards[:cut])
        return acts[which]

    def begin(found):
        for which in range(2):
            if acts[which] is None:
                early(which, found)
        first.extend(
            pl.pallas_call(
                functools.partial(first_kernel, tags[:cut], len(tags)),
                out_shape=(shape((frames, spots, chans), F32), shape((3, spots, chans), F32)),
                in_specs=[VMEM] * 4 + [SMEM, VMEM],
                out_specs=(VMEM, VMEM),
                compiler_params=params,
                name="first",
            )(*lats, *acts, clip_ids, w_time)
        )
        return first[1]

    if ringed:
        last = count // 4
        gates = {
            (1, 1, 1): lambda found: own,
            (1, last - 2, 1): lambda found: parts[1],
            (0, last - 1, 1): functools.partial(early, 0),
            (1, last - 1, 1): lambda found: found[9],
            (0, last, 0): functools.partial(early, 1),
            (0, last, 1): begin,
        }
        shards = gather_ring(shard, count, gates)
    else:
        whole = lax.all_gather(shard, "tm", axis=2, tiled=True)
        shards = [whole[:, :, :split], whole[:, :, split:]]
    if not first:
        begin(shards)
    rest, packet = first
    acts, packet = pl.pallas_call(
        functools.partial(late_kernel, tags[cut:], len(tags)),
        out_shape=(shape((frames, spots, chans - split), BF16), shape((3, spots, chans), BF16)),
        in_specs=[VMEM, VMEM, SMEM, VMEM, VMEM] + [VMEM] * (len(tags) - cut),
        out_specs=(VMEM, VMEM),
        compiler_params=params,
        name="late",
    )(*wides, clip_ids, w_time, packet, *shards[cut:])
    packet = lax.ppermute(packet, "tm", [(i, i + 1) for i in range(count - 1)])
    rest = pl.pallas_call(
        functools.partial(rest_kernel, tags[cut:], len(tags)),
        out_shape=shape((frames, spots, chans), F32),
        in_specs=[VMEM, SMEM, VMEM, VMEM],
        out_specs=VMEM,
        compiler_params=params,
        name="rest",
    )(acts, clip_ids, w_time, rest)
    return pl.pallas_call(
        attend_kernel,
        out_shape=shape((frames, rows, width, chans), BF16),
        in_specs=[VMEM, VMEM, SMEM, VMEM, VMEM, VMEM],
        out_specs=VMEM,
        scratch_shapes=[
            pltpu.VMEM((frames, height, width, chans), BF16),
            pltpu.VMEM((frames, height, width, chans), BF16),
        ],
        compiler_params=params,
        name="attend",
    )(rest, packet, clip_ids, gain_attn.reshape(1, chans), w_qkv, w_out)


def solution(mesh):
    placed = (P("tm", "rows", None, None), P(), P(), P(None, None, None, "tm"), P(), P(), P(), P())
    return jax.shard_map(
        local, mesh=mesh, in_specs=placed, out_specs=P("tm", "rows", None, None), check_vma=False
    )
```

```python
import functools

import jax
import jax.numpy as jnp
from jax import lax
from jax.experimental import pallas as pl
from jax.experimental.pallas import tpu as pltpu
from jax.sharding import PartitionSpec as P

LONGEST = 9
VMEM = pl.BlockSpec(memory_space=pltpu.VMEM)
SMEM = pl.BlockSpec(memory_space=pltpu.SMEM)
F32 = jnp.float32
BF16 = jnp.bfloat16


def dot(a, b):
    return jnp.dot(a, b, preferred_element_type=F32)


def dot_t(a, b):
    return lax.dot_general(a, b, (((1,), (1,)), ((), ())), preferred_element_type=F32)


def spot_of(device, count):
    z, y = device // 4, (device // 2) % 2
    return z + y * (count // 2 - 1 - 2 * z)


def device_at(spot, core, count):
    y = spot // (count // 4)
    return (spot + y * (count // 2 - 1 - 2 * spot)) * 4 + y * 2 + core


def ring_pairs(count):
    ring = count // 2
    pairs = []
    for spot in range(ring):
        pairs.append((device_at(spot, 0, count), device_at((spot + 1) % ring, 0, count)))
        pairs.append((device_at(spot, 1, count), device_at((spot - 1) % ring, 1, count)))
    return pairs


def ring_tags(count):
    tags = [(0, 0, 0), (0, 0, 1)]
    for step in range(1, count // 4 + 1):
        tags += [(step, 0, 0), (step, 1, 1)]
        if step < count // 4:
            tags += [(step, 0, 1), (step, 1, 0)]
    return tags


def after(shard, gate, found):
    if gate is None:
        return shard
    return lax.optimization_barrier((shard, gate(found)))[0]


def gather_ring(own, count, gates):
    ring = ring_pairs(count)
    cores = [(i, i ^ 1) for i in range(count)]
    last = count // 4
    found = [own, lax.ppermute(own, "tm", cores)]
    streams = list(found)
    for step in range(1, last + 1):
        for stream in range(2 if step < last else 1):
            shard = lax.ppermute(after(streams[stream], gates.get((stream, step, 0)), found), "tm", ring)
            streams[stream] = shard
            found.append(shard)
            found.append(lax.ppermute(after(shard, gates.get((stream, step, 1)), found), "tm", cores))
    return found


def shard_owner(tag, device, count):
    step, swapped, flip = tag
    core = device % 2
    ring = count // 2
    away = (1 - 2 * core) * ((1 - 2 * swapped) * step)
    spot = (spot_of(device, count) - away + ring) % ring
    return device_at(spot, (core + flip) % 2, count)


def normed_rows(raw, gain):
    rows, width, chans = raw.shape
    column = lax.broadcasted_iota(jnp.int32, (rows * width, 1), 0) % width
    x = raw.reshape(rows * width, chans).astype(F32)
    y = x * lax.rsqrt(jnp.mean(x * x, axis=-1, keepdims=True) + 1e-06) * gain
    before = jnp.where(column == 0, 0.0, pltpu.roll(y, 1, 0))
    after = jnp.where(column == width - 1, 0.0, pltpu.roll(y, rows * width - 1, 0))
    return [v.astype(BF16).reshape(rows, width, chans) for v in (before, y, after)]


def prepare_kernel(start, part_ref, gain_ref, band_ref):
    chans = part_ref.shape[-1]
    gain = gain_ref[...]
    for frame in range(band_ref.shape[0]):
        for dx, v in enumerate(normed_rows(part_ref[start + frame], gain)):
            band_ref[frame, :, :, dx * chans : (dx + 1) * chans] = v


def join_kernel(start, *refs):
    band_ref, *parts, gain_ref, wide_ref, lat_ref = refs
    frames, rows, width, wide = band_ref.shape
    chans = wide // 3
    groups = len(parts)
    mine = lax.axis_index("rows")
    gain = gain_ref[...]
    edge = jnp.zeros((width, wide), BF16)
    for at, part in enumerate(parts):
        first = at * rows
        if groups == 2:
            first = (mine if at == 0 else 1 - mine) * rows
        for frame in range(frames):
            raw = part[start + frame]
            lat_ref[frame, pl.ds(first, rows)] = raw
            if at == 0:
                wide_ref[frame, 0] = edge
                wide_ref[frame, groups * rows + 1] = edge
                wide_ref[frame, pl.ds(first + 1, rows)] = band_ref[frame]
                continue
            for dx, v in enumerate(normed_rows(raw, gain)):
                wide_ref[frame, pl.ds(first + 1, rows), :, dx * chans : (dx + 1) * chans] = v


def ordered(time_ref, tags, slots):
    block = time_ref.shape[1] // slots
    device = lax.axis_index("tm")
    rows = []
    for tag in tags:
        owner = shard_owner(tag, device, slots) if isinstance(tag, tuple) else tag
        rows.append(pl.ds(pl.multiple_of(owner * block, block), block))
    return [jnp.concatenate([time_ref[back, row] for row in rows], axis=0) for back in range(3)]


def convolve(wide_ref, shards):
    frames, height, width, wide = wide_ref.shape
    height -= 2
    total = None
    for dy in range(3):
        weights = jnp.concatenate(
            [jnp.concatenate([shard[dy, dx] for dx in range(3)], axis=-1) for shard in shards], axis=0
        )
        lhs = wide_ref[:, dy : dy + height].reshape(frames * height * width, wide)
        part = dot_t(lhs, weights)
        total = part if total is None else total + part
    acts = (total * jax.nn.sigmoid(total)).astype(BF16)
    return acts.reshape(frames, height * width, -1)


def keep(flag, values):
    return jnp.where(flag, values, jnp.zeros_like(values))


def temporal(acts, clips, weights, frames):
    first = lax.axis_index("tm") * frames
    spots, width = acts[0].shape
    lines = []
    for t in range(frames):
        line = [acts[t]]
        for back in (1, 2):
            if t < back:
                line.append(jnp.zeros((spots, width), BF16))
            else:
                line.append(keep(clips[first + t - back] == clips[first + t], acts[t - back]))
        lines.append(jnp.concatenate(line, axis=-1))
    lhs = jnp.concatenate(lines, axis=0)
    rhs = jnp.concatenate([weights[k] for k in range(3)], axis=0)
    return dot(lhs, rhs)


def packet_sums(acts, clips, weights, frames, lat=None):
    first = lax.axis_index("tm") * frames
    end = clips.shape[0] - 1
    next0 = clips[jnp.minimum(first + frames, end)]
    next1 = clips[jnp.minimum(first + frames + 1, end)]
    spots, width = acts[0].shape
    sums = [jnp.zeros((spots, width), F32) for _ in range(3)]
    base = None if lat is None else jnp.zeros(lat[0].shape, F32)
    for t in range(frames):
        inside = clips[first + t] == next0
        if lat is not None:
            base = base + keep(inside, lat[t].astype(F32))
        for back in range(min(3, t + 1)):
            both = jnp.logical_and(inside, clips[first + t - back] == next0)
            sums[back] = sums[back] + keep(both, acts[t - back].astype(F32))
    sums = [s.astype(BF16) for s in sums]
    last0 = keep(clips[first + frames - 1] == next0, acts[frames - 1])
    prev0 = keep(clips[first + frames - 2] == next0, acts[frames - 2])
    last1 = keep(clips[first + frames - 1] == next1, acts[frames - 1])
    by0 = dot(sums[0], weights[0])
    by1 = dot(jnp.concatenate([last0, sums[1]], axis=0), weights[1])
    by2 = dot(jnp.concatenate([prev0, last1, sums[2]], axis=0), weights[2])
    total = by0 + by1[spots:] + by2[2 * spots :]
    if base is not None:
        total = total + base
    return by1[:spots] + by2[:spots], by2[spots : 2 * spots], total


def early_kernel(wide_ref, *refs):
    *shards, acts_ref = refs
    acts_ref[...] = convolve(wide_ref, shards)


def first_kernel(tags, slots, lat0_ref, lat1_ref, acts0_ref, acts1_ref, clips, time_ref, rest_ref, packet_ref):
    weights = ordered(time_ref, tags, slots)
    acts = [ref[t] for ref in (acts0_ref, acts1_ref) for t in range(ref.shape[0])]
    lat = [ref[t].reshape(acts[0].shape[0], -1) for ref in (lat0_ref, lat1_ref) for t in range(ref.shape[0])]
    frames = len(acts)
    for i, part in enumerate(packet_sums(acts, clips, weights, frames, lat)):
        packet_ref[i] = part
    rest = temporal(acts, clips, weights, frames).reshape(rest_ref.shape)
    for t in range(frames):
        rest_ref[t] = rest[t] + lat[t].astype(F32)


def late_kernel(tags, slots, wide0_ref, wide1_ref, clips, time_ref, early_ref, *refs):
    *shards, acts_ref, packet_ref = refs
    half, frames = wide0_ref.shape[0], acts_ref.shape[0]
    acts_ref[:half] = convolve(wide0_ref, shards)
    acts_ref[half:] = convolve(wide1_ref, shards)
    acts = [acts_ref[t] for t in range(frames)]
    weights = ordered(time_ref, tags, slots)
    for i, part in enumerate(packet_sums(acts, clips, weights, frames)):
        packet_ref[i] = (early_ref[i] + part).astype(BF16)


def places(clips, frames):
    first = lax.axis_index("tm") * frames
    number = jnp.int32(1)
    for back in range(1, LONGEST):
        at = first - back
        hit = jnp.logical_and(at >= 0, clips[jnp.maximum(at, 0)] == clips[first])
        number = number + hit.astype(jnp.int32)
    found = [(None, clips[first] == clips[first], number)]
    for t in range(1, frames):
        same = clips[first + t] == clips[first + t - 1]
        number = jnp.where(same, number + 1, 1)
        found.append((same, clips[first + t] == clips[first], number))
    return found


def share(number, chans):
    return 1.0 / jnp.full((1, chans), number.astype(F32))


def rest_kernel(tags, slots, acts_ref, clips, time_ref, early_ref, base_ref):
    frames, spots, chans = base_ref.shape
    weights = ordered(time_ref, tags, slots)
    part = temporal([acts_ref[t] for t in range(frames)], clips, weights, frames)
    running = None
    for t, (same, _, number) in enumerate(places(clips, frames)):
        resid = early_ref[t] + part[t * spots : (t + 1) * spots]
        running = resid if t == 0 else keep(same, running) + resid
        base_ref[t] = resid + running * share(number, chans)


def attend_kernel(base_ref, packet_ref, clips, gain_ref, qkv_ref, proj_ref, out_ref, mixed_ref, normed_ref):
    frames, rows, width, chans = out_ref.shape
    height = mixed_ref.shape[1]
    spots = height * width
    own = rows * width
    mine = pl.ds(lax.axis_index("rows") * rows, rows)
    gain = gain_ref[...]
    place = places(clips, frames)
    step = frames // 2
    joint = 2 if spots <= 128 and step % 2 == 0 else 1
    blocked = (
        lax.broadcasted_iota(jnp.int32, (joint * own, joint * spots), 0) // own
        != lax.broadcasted_iota(jnp.int32, (joint * own, joint * spots), 1) // spots
    )

    terms = [packet_ref[0].astype(F32), packet_ref[1].astype(F32)]
    carried = packet_ref[2].astype(F32) + terms[0]
    for start in range(0, frames, step):
        for t in range(start, start + step):
            if t == 1:
                carried = carried + terms[1]
            _, among, number = place[t]
            mixed = base_ref[t] + carried * keep(among, share(number, chans))
            if t < 2:
                mixed = mixed + terms[t]
            mixed = mixed.astype(BF16)
            mixed_ref[t] = mixed.reshape(height, width, chans)
            x = mixed.astype(F32)
            y = x * lax.rsqrt(jnp.mean(x * x, axis=-1, keepdims=True) + 1e-06) * gain
            normed_ref[t] = y.astype(BF16).reshape(height, width, chans)
        span = slice(start, start + step)
        query = dot(normed_ref[span, mine].reshape(step * own, chans), qkv_ref[:, :chans]).astype(BF16)
        both = dot(normed_ref[span].reshape(step * spots, chans), qkv_ref[:, chans:]).astype(BF16)
        attended = []
        for t in range(0, step, joint):
            key = both[t * spots : (t + joint) * spots, :chans]
            value = both[t * spots : (t + joint) * spots, chans:]
            scores = dot_t(query[t * own : (t + joint) * own], key) * chans ** (-0.5)
            if joint > 1:
                scores = jnp.where(blocked, -jnp.inf, scores)
            weights = jnp.exp(scores - jnp.max(scores, axis=-1, keepdims=True))
            probs = (weights * (1.0 / jnp.sum(weights, axis=-1, keepdims=True))).astype(BF16)
            attended.append(dot(probs, value).astype(BF16))
        result = dot(jnp.concatenate(attended, axis=0), proj_ref[...])
        result = result + mixed_ref[span, mine].reshape(step * own, chans).astype(F32)
        out_ref[span] = result.astype(BF16).reshape(step, rows, width, chans)


def local(latents, clip_ids, gain_in, w_space, w_time, gain_attn, w_qkv, w_out):
    frames, rows, width, chans = latents.shape
    groups, count = lax.axis_size("rows"), lax.axis_size("tm")
    height = groups * rows
    spots = height * width
    shape = jax.ShapeDtypeStruct
    params = pltpu.CompilerParams(vmem_limit_bytes=(28 if frames * spots <= 1024 else 60) << 20)
    assert frames + 1 >= LONGEST

    half = frames // 2
    if groups == 2:
        parts = [latents, lax.ppermute(latents, "rows", [(0, 1), (1, 0)])]
    else:
        everything = lax.all_gather(latents, "rows")
        parts = [everything[i] for i in range(groups)]

    shard = jnp.transpose(w_space, (0, 1, 3, 2))
    ringed = shard.shape[2] % 16 == 0 and count % 8 == 0
    tags = ring_tags(count) if ringed else [0, 1]
    cut = len(tags) // 2
    split = cut * (chans // len(tags))

    gain = gain_in.reshape(1, chans)
    own = [
        pl.pallas_call(
            functools.partial(prepare_kernel, start),
            out_shape=shape((half, rows, width, 3 * chans), BF16),
            in_specs=[VMEM, VMEM],
            out_specs=VMEM,
            compiler_params=params,
            name="prepare",
        )(parts[0], gain)
        for start in (0, half)
    ]
    wides, lats = [None, None], [None, None]

    def join(which):
        wides[which], lats[which] = pl.pallas_call(
            functools.partial(join_kernel, which * half),
            out_shape=(
                shape((half, height + 2, width, 3 * chans), BF16),
                shape((half, height, width, chans), BF16),
            ),
            in_specs=[VMEM] * (groups + 2),
            out_specs=(VMEM, VMEM),
            compiler_params=params,
            name="join",
        )(own[which], *parts, gain)

    acts = [None, None]
    first = []

    def early(which, shards):
        join(which)
        acts[which] = pl.pallas_call(
            early_kernel,
            out_shape=shape((half, spots, split), BF16),
            in_specs=[VMEM] * (1 + cut),
            out_specs=VMEM,
            compiler_params=params,
            name="early",
        )(wides[which], *shards[:cut])
        return acts[which]

    def begin(found):
        for which in range(2):
            if acts[which] is None:
                early(which, found)
        first.extend(
            pl.pallas_call(
                functools.partial(first_kernel, tags[:cut], len(tags)),
                out_shape=(shape((frames, spots, chans), F32), shape((3, spots, chans), F32)),
                in_specs=[VMEM] * 4 + [SMEM, VMEM],
                out_specs=(VMEM, VMEM),
                compiler_params=params,
                name="first",
            )(*lats, *acts, clip_ids, w_time)
        )
        return first[1]

    if ringed:
        last = count // 4
        gates = {
            (1, 1, 1): lambda found: own,
            (1, last - 2, 1): lambda found: parts[1],
            (0, last - 1, 1): functools.partial(early, 0),
            (1, last - 1, 1): lambda found: found[9],
            (0, last, 0): functools.partial(early, 1),
            (0, last, 1): begin,
        }
        shards = gather_ring(shard, count, gates)
    else:
        whole = lax.all_gather(shard, "tm", axis=2, tiled=True)
        shards = [whole[:, :, :split], whole[:, :, split:]]
    if not first:
        begin(shards)
    rest, packet = first
    acts, packet = pl.pallas_call(
        functools.partial(late_kernel, tags[cut:], len(tags)),
        out_shape=(shape((frames, spots, chans - split), BF16), shape((3, spots, chans), BF16)),
        in_specs=[VMEM, VMEM, SMEM, VMEM, VMEM] + [VMEM] * (len(tags) - cut),
        out_specs=(VMEM, VMEM),
        compiler_params=params,
        name="late",
    )(*wides, clip_ids, w_time, packet, *shards[cut:])
    packet = lax.ppermute(packet, "tm", [(i, i + 1) for i in range(count - 1)])
    rest = pl.pallas_call(
        functools.partial(rest_kernel, tags[cut:], len(tags)),
        out_shape=shape((frames, spots, chans), F32),
        in_specs=[VMEM, SMEM, VMEM, VMEM],
        out_specs=VMEM,
        compiler_params=params,
        name="rest",
    )(acts, clip_ids, w_time, rest)
    return pl.pallas_call(
        attend_kernel,
        out_shape=shape((frames, rows, width, chans), BF16),
        in_specs=[VMEM, VMEM, SMEM, VMEM, VMEM, VMEM],
        out_specs=VMEM,
        scratch_shapes=[
            pltpu.VMEM((frames, height, width, chans), BF16),
            pltpu.VMEM((frames, height, width, chans), BF16),
        ],
        compiler_params=params,
        name="attend",
    )(rest, packet, clip_ids, gain_attn.reshape(1, chans), w_qkv, w_out)


def solution(mesh):
    placed = (P("tm", "rows", None, None), P(), P(), P(None, None, None, "tm"), P(), P(), P(), P())
    return jax.shard_map(
        local, mesh=mesh, in_specs=placed, out_specs=P("tm", "rows", None, None), check_vma=False
    )
```

```python
import functools

import jax
import jax.numpy as jnp
from jax import lax
from jax.experimental import pallas as pl
from jax.experimental.pallas import tpu as pltpu
from jax.sharding import PartitionSpec as P

LONGEST = 9
VMEM = pl.BlockSpec(memory_space=pltpu.VMEM)
SMEM = pl.BlockSpec(memory_space=pltpu.SMEM)
F32 = jnp.float32
BF16 = jnp.bfloat16


def dot(a, b):
    return jnp.dot(a, b, preferred_element_type=F32)


def dot_t(a, b):
    return lax.dot_general(a, b, (((1,), (1,)), ((), ())), preferred_element_type=F32)


def spot_of(device, count):
    z, y = device // 4, (device // 2) % 2
    return z + y * (count // 2 - 1 - 2 * z)


def device_at(spot, core, count):
    y = spot // (count // 4)
    return (spot + y * (count // 2 - 1 - 2 * spot)) * 4 + y * 2 + core


def ring_pairs(count):
    ring = count // 2
    pairs = []
    for spot in range(ring):
        pairs.append((device_at(spot, 0, count), device_at((spot + 1) % ring, 0, count)))
        pairs.append((device_at(spot, 1, count), device_at((spot - 1) % ring, 1, count)))
    return pairs


def ring_tags(count):
    tags = [(0, 0, 0), (0, 0, 1)]
    for step in range(1, count // 4 + 1):
        tags += [(step, 0, 0), (step, 1, 1)]
        if step < count // 4:
            tags += [(step, 0, 1), (step, 1, 0)]
    return tags


def after(shard, gate, found):
    if gate is None:
        return shard
    return lax.optimization_barrier((shard, gate(found)))[0]


def gather_ring(own, count, gates):
    ring = ring_pairs(count)
    cores = [(i, i ^ 1) for i in range(count)]
    last = count // 4
    found = [own, lax.ppermute(own, "tm", cores)]
    streams = list(found)
    for step in range(1, last + 1):
        for stream in range(2 if step < last else 1):
            shard = lax.ppermute(after(streams[stream], gates.get((stream, step, 0)), found), "tm", ring)
            streams[stream] = shard
            found.append(shard)
            found.append(lax.ppermute(after(shard, gates.get((stream, step, 1)), found), "tm", cores))
    return found


def shard_owner(tag, device, count):
    step, swapped, flip = tag
    core = device % 2
    ring = count // 2
    away = (1 - 2 * core) * ((1 - 2 * swapped) * step)
    spot = (spot_of(device, count) - away + ring) % ring
    return device_at(spot, (core + flip) % 2, count)


def normed_rows(raw, gain):
    rows, width, chans = raw.shape
    column = lax.broadcasted_iota(jnp.int32, (rows * width, 1), 0) % width
    x = raw.reshape(rows * width, chans).astype(F32)
    y = x * lax.rsqrt(jnp.mean(x * x, axis=-1, keepdims=True) + 1e-06) * gain
    before = jnp.where(column == 0, 0.0, pltpu.roll(y, 1, 0))
    after = jnp.where(column == width - 1, 0.0, pltpu.roll(y, rows * width - 1, 0))
    return [v.astype(BF16).reshape(rows, width, chans) for v in (before, y, after)]


def prepare_kernel(start, part_ref, gain_ref, band_ref):
    chans = part_ref.shape[-1]
    gain = gain_ref[...]
    for frame in range(band_ref.shape[0]):
        for dx, v in enumerate(normed_rows(part_ref[start + frame], gain)):
            band_ref[frame, :, :, dx * chans : (dx + 1) * chans] = v


def join_kernel(start, *refs):
    band_ref, *parts, gain_ref, wide_ref, lat_ref = refs
    frames, rows, width, wide = band_ref.shape
    chans = wide // 3
    groups = len(parts)
    mine = lax.axis_index("rows")
    gain = gain_ref[...]
    edge = jnp.zeros((width, wide), BF16)
    for at, part in enumerate(parts):
        first = at * rows
        if groups == 2:
            first = (mine if at == 0 else 1 - mine) * rows
        for frame in range(frames):
            raw = part[start + frame]
            lat_ref[frame, pl.ds(first, rows)] = raw
            if at == 0:
                wide_ref[frame, 0] = edge
                wide_ref[frame, groups * rows + 1] = edge
                wide_ref[frame, pl.ds(first + 1, rows)] = band_ref[frame]
                continue
            for dx, v in enumerate(normed_rows(raw, gain)):
                wide_ref[frame, pl.ds(first + 1, rows), :, dx * chans : (dx + 1) * chans] = v


def ordered(time_ref, tags, slots):
    block = time_ref.shape[1] // slots
    device = lax.axis_index("tm")
    rows = []
    for tag in tags:
        owner = shard_owner(tag, device, slots) if isinstance(tag, tuple) else tag
        rows.append(pl.ds(pl.multiple_of(owner * block, block), block))
    return [jnp.concatenate([time_ref[back, row] for row in rows], axis=0) for back in range(3)]


def convolve(wide_ref, shards):
    frames, height, width, wide = wide_ref.shape
    height -= 2
    total = None
    for dy in range(3):
        weights = jnp.concatenate(
            [jnp.concatenate([shard[dy, dx] for dx in range(3)], axis=-1) for shard in shards], axis=0
        )
        lhs = wide_ref[:, dy : dy + height].reshape(frames * height * width, wide)
        part = dot_t(lhs, weights)
        total = part if total is None else total + part
    acts = (total * jax.nn.sigmoid(total)).astype(BF16)
    return acts.reshape(frames, height * width, -1)


def keep(flag, values):
    return jnp.where(flag, values, jnp.zeros_like(values))


def temporal(acts, clips, weights, frames):
    first = lax.axis_index("tm") * frames
    spots, width = acts[0].shape
    lines = []
    for t in range(frames):
        line = [acts[t]]
        for back in (1, 2):
            if t < back:
                line.append(jnp.zeros((spots, width), BF16))
            else:
                line.append(keep(clips[first + t - back] == clips[first + t], acts[t - back]))
        lines.append(jnp.concatenate(line, axis=-1))
    lhs = jnp.concatenate(lines, axis=0)
    rhs = jnp.concatenate([weights[k] for k in range(3)], axis=0)
    return dot(lhs, rhs)


def packet_sums(acts, clips, weights, frames, lat=None):
    first = lax.axis_index("tm") * frames
    end = clips.shape[0] - 1
    next0 = clips[jnp.minimum(first + frames, end)]
    next1 = clips[jnp.minimum(first + frames + 1, end)]
    spots, width = acts[0].shape
    sums = [jnp.zeros((spots, width), F32) for _ in range(3)]
    base = None if lat is None else jnp.zeros(lat[0].shape, F32)
    for t in range(frames):
        inside = clips[first + t] == next0
        if lat is not None:
            base = base + keep(inside, lat[t].astype(F32))
        for back in range(min(3, t + 1)):
            both = jnp.logical_and(inside, clips[first + t - back] == next0)
            sums[back] = sums[back] + keep(both, acts[t - back].astype(F32))
    sums = [s.astype(BF16) for s in sums]
    last0 = keep(clips[first + frames - 1] == next0, acts[frames - 1])
    prev0 = keep(clips[first + frames - 2] == next0, acts[frames - 2])
    last1 = keep(clips[first + frames - 1] == next1, acts[frames - 1])
    by0 = dot(sums[0], weights[0])
    by1 = dot(jnp.concatenate([last0, sums[1]], axis=0), weights[1])
    by2 = dot(jnp.concatenate([prev0, last1, sums[2]], axis=0), weights[2])
    total = by0 + by1[spots:] + by2[2 * spots :]
    if base is not None:
        total = total + base
    return by1[:spots] + by2[:spots], by2[spots : 2 * spots], total


def early_kernel(wide_ref, *refs):
    *shards, acts_ref = refs
    acts_ref[...] = convolve(wide_ref, shards)


def first_kernel(tags, slots, lat0_ref, lat1_ref, acts0_ref, acts1_ref, clips, time_ref, rest_ref, packet_ref):
    weights = ordered(time_ref, tags, slots)
    acts = [ref[t] for ref in (acts0_ref, acts1_ref) for t in range(ref.shape[0])]
    lat = [ref[t].reshape(acts[0].shape[0], -1) for ref in (lat0_ref, lat1_ref) for t in range(ref.shape[0])]
    frames = len(acts)
    for i, part in enumerate(packet_sums(acts, clips, weights, frames, lat)):
        packet_ref[i] = part
    rest = temporal(acts, clips, weights, frames).reshape(rest_ref.shape)
    for t in range(frames):
        rest_ref[t] = rest[t] + lat[t].astype(F32)


def late_kernel(tags, slots, wide0_ref, wide1_ref, clips, time_ref, early_ref, *refs):
    *shards, acts_ref, packet_ref = refs
    half, frames = wide0_ref.shape[0], acts_ref.shape[0]
    acts_ref[:half] = convolve(wide0_ref, shards)
    acts_ref[half:] = convolve(wide1_ref, shards)
    acts = [acts_ref[t] for t in range(frames)]
    weights = ordered(time_ref, tags, slots)
    for i, part in enumerate(packet_sums(acts, clips, weights, frames)):
        packet_ref[i] = (early_ref[i] + part).astype(BF16)


def places(clips, frames):
    first = lax.axis_index("tm") * frames
    number = jnp.int32(1)
    for back in range(1, LONGEST):
        at = first - back
        hit = jnp.logical_and(at >= 0, clips[jnp.maximum(at, 0)] == clips[first])
        number = number + hit.astype(jnp.int32)
    found = [(None, clips[first] == clips[first], number)]
    for t in range(1, frames):
        same = clips[first + t] == clips[first + t - 1]
        number = jnp.where(same, number + 1, 1)
        found.append((same, clips[first + t] == clips[first], number))
    return found


def share(number, chans):
    return 1.0 / jnp.full((1, chans), number.astype(F32))


def rest_kernel(tags, slots, acts_ref, clips, time_ref, early_ref, base_ref):
    frames, spots, chans = base_ref.shape
    weights = ordered(time_ref, tags, slots)
    part = temporal([acts_ref[t] for t in range(frames)], clips, weights, frames)
    running = None
    for t, (same, _, number) in enumerate(places(clips, frames)):
        resid = early_ref[t] + part[t * spots : (t + 1) * spots]
        running = resid if t == 0 else keep(same, running) + resid
        base_ref[t] = resid + running * share(number, chans)


def attend_kernel(base_ref, packet_ref, clips, gain_ref, qkv_ref, proj_ref, out_ref, mixed_ref, normed_ref):
    frames, rows, width, chans = out_ref.shape
    height = mixed_ref.shape[1]
    spots = height * width
    own = rows * width
    mine = pl.ds(lax.axis_index("rows") * rows, rows)
    gain = gain_ref[...]
    place = places(clips, frames)
    step = frames // 2
    joint = 2 if spots <= 128 and step % 2 == 0 else 1
    blocked = (
        lax.broadcasted_iota(jnp.int32, (joint * own, joint * spots), 0) // own
        != lax.broadcasted_iota(jnp.int32, (joint * own, joint * spots), 1) // spots
    )

    terms = [packet_ref[0].astype(F32), packet_ref[1].astype(F32)]
    carried = packet_ref[2].astype(F32) + terms[0]
    for start in range(0, frames, step):
        for t in range(start, start + step):
            if t == 1:
                carried = carried + terms[1]
            _, among, number = place[t]
            mixed = base_ref[t] + carried * keep(among, share(number, chans))
            if t < 2:
                mixed = mixed + terms[t]
            mixed = mixed.astype(BF16)
            mixed_ref[t] = mixed.reshape(height, width, chans)
            x = mixed.astype(F32)
            y = x * lax.rsqrt(jnp.mean(x * x, axis=-1, keepdims=True) + 1e-06) * gain
            normed_ref[t] = y.astype(BF16).reshape(height, width, chans)
        span = slice(start, start + step)
        query = dot(normed_ref[span, mine].reshape(step * own, chans), qkv_ref[:, :chans]).astype(BF16)
        both = dot(normed_ref[span].reshape(step * spots, chans), qkv_ref[:, chans:]).astype(BF16)
        attended = []
        for t in range(0, step, joint):
            key = both[t * spots : (t + joint) * spots, :chans]
            value = both[t * spots : (t + joint) * spots, chans:]
            scores = dot_t(query[t * own : (t + joint) * own], key) * chans ** (-0.5)
            if joint > 1:
                scores = jnp.where(blocked, -jnp.inf, scores)
            weights = jnp.exp(scores - jnp.max(scores, axis=-1, keepdims=True))
            probs = (weights * (1.0 / jnp.sum(weights, axis=-1, keepdims=True))).astype(BF16)
            attended.append(dot(probs, value).astype(BF16))
        result = dot(jnp.concatenate(attended, axis=0), proj_ref[...])
        result = result + mixed_ref[span, mine].reshape(step * own, chans).astype(F32)
        out_ref[span] = result.astype(BF16).reshape(step, rows, width, chans)


def local(latents, clip_ids, gain_in, w_space, w_time, gain_attn, w_qkv, w_out):
    frames, rows, width, chans = latents.shape
    groups, count = lax.axis_size("rows"), lax.axis_size("tm")
    height = groups * rows
    spots = height * width
    shape = jax.ShapeDtypeStruct
    params = pltpu.CompilerParams(vmem_limit_bytes=(28 if frames * spots <= 1024 else 60) << 20)
    assert frames + 1 >= LONGEST

    half = frames // 2
    if groups == 2:
        parts = [latents, lax.ppermute(latents, "rows", [(0, 1), (1, 0)])]
    else:
        everything = lax.all_gather(latents, "rows")
        parts = [everything[i] for i in range(groups)]

    shard = jnp.transpose(w_space, (0, 1, 3, 2))
    ringed = shard.shape[2] % 16 == 0 and count % 8 == 0
    tags = ring_tags(count) if ringed else [0, 1]
    cut = len(tags) // 2
    split = cut * (chans // len(tags))

    gain = gain_in.reshape(1, chans)
    own = [
        pl.pallas_call(
            functools.partial(prepare_kernel, start),
            out_shape=shape((half, rows, width, 3 * chans), BF16),
            in_specs=[VMEM, VMEM],
            out_specs=VMEM,
            compiler_params=params,
            name="prepare",
        )(parts[0], gain)
        for start in (0, half)
    ]
    wides, lats = [None, None], [None, None]

    def join(which):
        wides[which], lats[which] = pl.pallas_call(
            functools.partial(join_kernel, which * half),
            out_shape=(
                shape((half, height + 2, width, 3 * chans), BF16),
                shape((half, height, width, chans), BF16),
            ),
            in_specs=[VMEM] * (groups + 2),
            out_specs=(VMEM, VMEM),
            compiler_params=params,
            name="join",
        )(own[which], *parts, gain)

    acts = [None, None]
    first = []

    def early(which, shards):
        join(which)
        acts[which] = pl.pallas_call(
            early_kernel,
            out_shape=shape((half, spots, split), BF16),
            in_specs=[VMEM] * (1 + cut),
            out_specs=VMEM,
            compiler_params=params,
            name="early",
        )(wides[which], *shards[:cut])
        return acts[which]

    def begin(found):
        for which in range(2):
            if acts[which] is None:
                early(which, found)
        first.extend(
            pl.pallas_call(
                functools.partial(first_kernel, tags[:cut], len(tags)),
                out_shape=(shape((frames, spots, chans), F32), shape((3, spots, chans), F32)),
                in_specs=[VMEM] * 4 + [SMEM, VMEM],
                out_specs=(VMEM, VMEM),
                compiler_params=params,
                name="first",
            )(*lats, *acts, clip_ids, w_time)
        )
        return first[1]

    if ringed:
        last = count // 4
        gates = {
            (1, 1, 1): lambda found: own,
            (0, last - 1, 1): functools.partial(early, 0),
            (1, last - 1, 1): lambda found: found[9],
            (0, last, 0): functools.partial(early, 1),
        }
        shards = gather_ring(shard, count, gates)
    else:
        whole = lax.all_gather(shard, "tm", axis=2, tiled=True)
        shards = [whole[:, :, :split], whole[:, :, split:]]
    if not first:
        begin(shards)
    rest, packet = first
    acts, packet = pl.pallas_call(
        functools.partial(late_kernel, tags[cut:], len(tags)),
        out_shape=(shape((frames, spots, chans - split), BF16), shape((3, spots, chans), BF16)),
        in_specs=[VMEM, VMEM, SMEM, VMEM, VMEM] + [VMEM] * (len(tags) - cut),
        out_specs=(VMEM, VMEM),
        compiler_params=params,
        name="late",
    )(*wides, clip_ids, w_time, packet, *shards[cut:])
    packet = lax.ppermute(packet, "tm", [(i, i + 1) for i in range(count - 1)])
    rest = pl.pallas_call(
        functools.partial(rest_kernel, tags[cut:], len(tags)),
        out_shape=shape((frames, spots, chans), F32),
        in_specs=[VMEM, SMEM, VMEM, VMEM],
        out_specs=VMEM,
        compiler_params=params,
        name="rest",
    )(acts, clip_ids, w_time, rest)
    return pl.pallas_call(
        attend_kernel,
        out_shape=shape((frames, rows, width, chans), BF16),
        in_specs=[VMEM, VMEM, SMEM, VMEM, VMEM, VMEM],
        out_specs=VMEM,
        scratch_shapes=[
            pltpu.VMEM((frames, height, width, chans), BF16),
            pltpu.VMEM((frames, height, width, chans), BF16),
        ],
        compiler_params=params,
        name="attend",
    )(rest, packet, clip_ids, gain_attn.reshape(1, chans), w_qkv, w_out)


def solution(mesh):
    placed = (P("tm", "rows", None, None), P(), P(), P(None, None, None, "tm"), P(), P(), P(), P())
    return jax.shard_map(
        local, mesh=mesh, in_specs=placed, out_specs=P("tm", "rows", None, None), check_vma=False
    )
```
